128 devices in a mesh: sample: 16 (over y, x), col: 8 (over z, core).
Axes of the slice: x: 4, y: 4, z: 4, core: 2. Of those that a mesh axis runs over, the one named last changes fastest.
Arguments:
- block_inputs: bfloat16 [2048, 17, 17, 768], P(('sample', 'col')), may hold values from 0 to 100, as said below
- first_entry: bfloat16 [1, 1, 768, 384], replicated, may hold values from -0.3125 to 0.3125
- first_wide: bfloat16 [3, 3, 192, 320], replicated, may hold values from -0.21875 to 0.21875
- first_row: bfloat16 [1, 7, 192, 192], replicated, may hold values from -0.25 to 0.25
- first_column: bfloat16 [7, 1, 192, 192], replicated, may hold values from -0.25 to 0.25
- first_reduce: bfloat16 [3, 3, 192, 192], replicated, may hold values from -0.21875 to 0.21875
- second_entry: bfloat16 [1, 1, 1280, 1152], replicated, may hold values from -0.25 to 0.25
- second_row: bfloat16 [1, 3, 384, 384], replicated, may hold values from -0.25 to 0.25
- second_column: bfloat16 [3, 1, 384, 384], replicated, may hold values from -0.25 to 0.25
- second_deep: bfloat16 [3, 3, 448, 384], replicated, may hold values from -0.125 to 0.125
- deep_row: bfloat16 [1, 3, 384, 384], replicated, may hold values from -0.25 to 0.25
- deep_column: bfloat16 [3, 1, 384, 384], replicated, may hold values from -0.25 to 0.25
- pool_project: bfloat16 [1, 1, 1280, 192], replicated, may hold values from -0.25 to 0.25
Outputs:
- feature_mean: float32 [2048], replicated
- covariance: float32 [2048, 2048], P('sample', 'col')
The draws below stay inside these ranges and needn't reach their ends.
Inputs may be any that keep to these rules, and one draw needn't show every extreme that they name: `block_inputs`: nonnegative activations.
All inputs are finite; a program needn't handle non-finite values.
Results may differ from the reference program's by a relative error of at most 0.0003.
Values sent between devices are 32-bit elements; how exact they have to be, the bound alone decides.
No kernel may reach another device: no remote copies, remote signals or barrier semaphores. Data moves between devices by JAX's collectives and lax.ppermute only.
A program may use at most 128 MiB of HBM per device.

```python
import math
import jax
import jax.numpy as jnp
from jax import lax

GRID = 17
IN_CH = 768
RED_CH = 192
WIDE_CH = 320
BR_CH = 384
DEEP_CH = 448
POOL_CH = 192
MID_CH = 1280
FEAT = 2048
IMAGES = 2048
N_COL = 8


def draw_block_inputs(key, part):
    keys = jax.random.split(key, 5)
    index = jnp.arange(IMAGES).astype(jnp.float32)
    position = index / max(IMAGES - 1, 1)
    spread = jnp.exp(jax.random.uniform(keys[0], (IMAGES,), jnp.float32, 0.0, math.log(3.4)))
    channel = jnp.exp(jax.random.uniform(keys[1], (IN_CH,), jnp.float32, math.log(0.5), math.log(2.0)))
    shape = (IMAGES, GRID, GRID, IN_CH)
    trend = jnp.exp(position * math.log(3.0))
    values = jnp.clip(jnp.abs(jax.random.normal(keys[4], shape, jnp.float32)), 0.0, 6.0)
    scale = trend * spread * 0.25
    return (values * scale[:, None, None, None] * channel).astype(jnp.bfloat16)


def gaussian(own_key, extent, deviation, limit, kind=jnp.bfloat16):
    values = jax.random.normal(own_key, extent, jnp.float32) * deviation
    return jnp.minimum(jnp.maximum(values, -limit), limit).astype(kind)


def setup_inputs(seed: int = 0) -> dict:
    key_list = jax.random.split(jax.random.key(seed), 14)
    return {
        "block_inputs": draw_block_inputs(jax.random.fold_in(key_list[13], 71), 0),
        "first_entry": gaussian(key_list[1], (1, 1, IN_CH, 2 * RED_CH), (IN_CH // 2) ** -0.5, 0.3125),
        "first_wide": gaussian(key_list[2], (3, 3, RED_CH, WIDE_CH), (9 * RED_CH // 2) ** -0.5, 0.21875),
        "first_row": gaussian(key_list[3], (1, 7, RED_CH, RED_CH), (7 * RED_CH // 2) ** -0.5, 0.25),
        "first_column": gaussian(key_list[4], (7, 1, RED_CH, RED_CH), (7 * RED_CH // 2) ** -0.5, 0.25),
        "first_reduce": gaussian(key_list[5], (3, 3, RED_CH, RED_CH), (9 * RED_CH // 2) ** -0.5, 0.21875),
        "second_entry": gaussian(key_list[6], (1, 1, MID_CH, WIDE_CH + BR_CH + DEEP_CH), (MID_CH // 2) ** -0.5, 0.25),
        "second_row": gaussian(key_list[7], (1, 3, BR_CH, BR_CH), (3 * BR_CH // 2) ** -0.5, 0.25),
        "second_column": gaussian(key_list[8], (3, 1, BR_CH, BR_CH), (3 * BR_CH // 2) ** -0.5, 0.25),
        "second_deep": gaussian(key_list[9], (3, 3, DEEP_CH, BR_CH), (9 * DEEP_CH // 2) ** -0.5, 0.125),
        "deep_row": gaussian(key_list[10], (1, 3, BR_CH, BR_CH), (3 * BR_CH // 2) ** -0.5, 0.25),
        "deep_column": gaussian(key_list[11], (3, 1, BR_CH, BR_CH), (3 * BR_CH // 2) ** -0.5, 0.25),
        "pool_project": gaussian(key_list[12], (1, 1, MID_CH, POOL_CH), (MID_CH // 2) ** -0.5, 0.25),
    }


def rectify(inputs, kernel, stride, padding):
    result = lax.conv_general_dilated(inputs, kernel, (stride, stride), padding, dimension_numbers=("NHWC", "HWIO", "NHWC"), preferred_element_type=jnp.float32)
    return jnp.maximum(result, 0.0).astype(jnp.bfloat16)


def spatial_mean(inputs):
    return jnp.mean(inputs.astype(jnp.float32), axis=(1, 2))


def network(block_inputs, first_entry, first_wide, first_row, first_column, first_reduce, second_entry, second_row, second_column, second_deep, deep_row, deep_column, pool_project):
    no_margin = ((0, 0), (0, 0))
    entry_out = rectify(block_inputs, first_entry, 1, no_margin)
    half_width = first_wide.shape[2]
    wide_out = rectify(entry_out[..., :half_width], first_wide, 2, no_margin)
    tower_out = rectify(entry_out[..., half_width:], first_row, 1, ((0, 0), (3, 3)))
    tower_out = rectify(tower_out, first_column, 1, ((3, 3), (0, 0)))
    tower_out = rectify(tower_out, first_reduce, 2, no_margin)
    maximum = lax.reduce_window(block_inputs, jnp.array(-jnp.inf, block_inputs.dtype), lax.max, (1, 3, 3, 1), (1, 2, 2, 1), "VALID")
    middle = jnp.concatenate([wide_out, tower_out, maximum], axis=3)
    second = rectify(middle, second_entry, 1, no_margin)
    branch_width = second_row.shape[2]
    deep_width = second_deep.shape[2]
    plain_width = second_entry.shape[3] - branch_width - deep_width
    plain_out = second[..., :plain_width]
    branch_in = second[..., plain_width:plain_width + branch_width]
    deep_in = second[..., plain_width + branch_width:]
    row_a = rectify(branch_in, second_row, 1, ((0, 0), (1, 1)))
    col_a = rectify(branch_in, second_column, 1, ((1, 1), (0, 0)))
    deep_out = rectify(deep_in, second_deep, 1, ((1, 1), (1, 1)))
    row_b = rectify(deep_out, deep_row, 1, ((0, 0), (1, 1)))
    col_b = rectify(deep_out, deep_column, 1, ((1, 1), (0, 0)))
    pool_pad = ((0, 0), (1, 1), (1, 1), (0, 0))
    summed = lax.reduce_window(middle.astype(jnp.float32), jnp.array(0.0, jnp.float32), lax.add, (1, 3, 3, 1), (1, 1, 1, 1), pool_pad)
    ones_map = jnp.ones((1, middle.shape[1], middle.shape[2], 1), jnp.float32)
    cell_count = lax.reduce_window(ones_map, jnp.array(0.0, jnp.float32), lax.add, (1, 3, 3, 1), (1, 1, 1, 1), pool_pad)
    averaged = (summed / cell_count).astype(jnp.bfloat16)
    pooled = rectify(averaged, pool_project, 1, no_margin)
    return jnp.concatenate([spatial_mean(plain_out), spatial_mean(row_a), spatial_mean(col_a), spatial_mean(row_b), spatial_mean(col_b), spatial_mean(pooled)], axis=1)


def reference(block_inputs, first_entry, first_wide, first_row, first_column, first_reduce, second_entry, second_row, second_column, second_deep, deep_row, deep_column, pool_project):
    batches = block_inputs.reshape((IMAGES // N_COL, N_COL) + block_inputs.shape[1:])

    def one_batch(images):
        return network(images, first_entry, first_wide, first_row, first_column, first_reduce, second_entry, second_row, second_column, second_deep, deep_row, deep_column, pool_project)

    features = lax.map(one_batch, batches).reshape((IMAGES, FEAT))
    feature_mean = jnp.sum(features, axis=0) / IMAGES
    centered = features - feature_mean
    covariance = jnp.einsum("nf,ng->fg", centered, centered, precision=lax.Precision.HIGHEST, preferred_element_type=jnp.float32) / (IMAGES - 1)
    return (feature_mean, covariance)
```

```python
import jax
import jax.numpy as jnp
from jax import lax
from jax.sharding import Mesh, PartitionSpec as P

AXES = ("y", "xh", "xl", "z", "core")
IMAGES = 2048
FEAT = 2048
LOCAL = 16
GROUP = 512


def rectify(inputs, kernel, stride, padding):
    result = lax.conv_general_dilated(
        inputs,
        kernel,
        (stride, stride),
        padding,
        dimension_numbers=("NHWC", "HWIO", "NHWC"),
        preferred_element_type=jnp.float32,
    )
    return jnp.maximum(result, 0.0).astype(jnp.bfloat16)


def spatial_mean(inputs):
    return jnp.mean(inputs.astype(jnp.float32), axis=(1, 2))


def network(
    block_inputs,
    first_entry,
    first_wide,
    first_row,
    first_column,
    first_reduce,
    second_entry,
    second_row,
    second_column,
    second_deep,
    deep_row,
    deep_column,
    pool_project,
):
    no_margin = ((0, 0), (0, 0))
    entry_out = rectify(block_inputs, first_entry, 1, no_margin)
    half_width = first_wide.shape[2]
    wide_out = rectify(entry_out[..., :half_width], first_wide, 2, no_margin)
    tower_out = rectify(entry_out[..., half_width:], first_row, 1, ((0, 0), (3, 3)))
    tower_out = rectify(tower_out, first_column, 1, ((3, 3), (0, 0)))
    tower_out = rectify(tower_out, first_reduce, 2, no_margin)
    maximum = lax.reduce_window(
        block_inputs,
        jnp.array(-jnp.inf, block_inputs.dtype),
        lax.max,
        (1, 3, 3, 1),
        (1, 2, 2, 1),
        "VALID",
    )
    middle = jnp.concatenate([wide_out, tower_out, maximum], axis=3)
    second = rectify(middle, second_entry, 1, no_margin)
    branch_width = second_row.shape[2]
    deep_width = second_deep.shape[2]
    plain_width = second_entry.shape[3] - branch_width - deep_width
    plain_out = second[..., :plain_width]
    branch_in = second[..., plain_width : plain_width + branch_width]
    deep_in = second[..., plain_width + branch_width :]
    row_a = rectify(branch_in, second_row, 1, ((0, 0), (1, 1)))
    col_a = rectify(branch_in, second_column, 1, ((1, 1), (0, 0)))
    deep_out = rectify(deep_in, second_deep, 1, ((1, 1), (1, 1)))
    row_b = rectify(deep_out, deep_row, 1, ((0, 0), (1, 1)))
    col_b = rectify(deep_out, deep_column, 1, ((1, 1), (0, 0)))
    pool_pad = ((0, 0), (1, 1), (1, 1), (0, 0))
    summed = lax.reduce_window(
        middle.astype(jnp.float32),
        jnp.array(0.0, jnp.float32),
        lax.add,
        (1, 3, 3, 1),
        (1, 1, 1, 1),
        pool_pad,
    )
    ones_map = jnp.ones((1, middle.shape[1], middle.shape[2], 1), jnp.float32)
    cell_count = lax.reduce_window(
        ones_map, jnp.array(0.0, jnp.float32), lax.add, (1, 3, 3, 1), (1, 1, 1, 1), pool_pad
    )
    averaged = (summed / cell_count).astype(jnp.bfloat16)
    pooled = rectify(averaged, pool_project, 1, no_margin)
    return jnp.concatenate(
        [
            spatial_mean(plain_out),
            spatial_mean(row_a),
            spatial_mean(col_a),
            spatial_mean(row_b),
            spatial_mean(col_b),
            spatial_mean(pooled),
        ],
        axis=1,
    )


def cut(array, index, size, axis):
    return lax.dynamic_slice_in_dim(array, index * size, size, axis)


def statistics(features):
    highest = lax.Precision.HIGHEST
    x = lax.axis_index("xh") * 2 + lax.axis_index("xl")
    core = lax.axis_index("core")
    row_block = lax.axis_index("y") * 4 + x
    col_block = lax.axis_index("z") * 2 + core
    rows = features.reshape(LOCAL, 4, 4, 128).transpose(2, 0, 1, 3).reshape(4, 1, LOCAL, 512)
    columns = features.reshape(LOCAL, 4, 512).transpose(1, 0, 2)[None]
    sums = jnp.sum(features, axis=0).reshape(1, 1, LOCAL, 128)
    message = jnp.concatenate(
        [
            jnp.broadcast_to(rows, (4, 4, LOCAL, 512)),
            jnp.broadcast_to(columns, (4, 4, LOCAL, 512)),
            jnp.broadcast_to(sums, (4, 4, LOCAL, 128)),
        ],
        axis=-1,
    ).reshape(16, LOCAL, 1152)
    got = lax.all_to_all(message, ("xh", "xl", "z"), 0, 0, tiled=True)
    half_sum = jnp.sum(got[:, :, 1024:], axis=0)
    other_columns = lax.dynamic_slice_in_dim(got, 512 + 256 * (1 - core), 256, 2)
    pass_on = jnp.concatenate([got[:, :, :512], other_columns], -1).reshape(256, 768)
    pass_on = jnp.concatenate(
        [pass_on, jnp.pad(half_sum, ((0, 0), (0, 640)))], 0
    )
    passed = lax.ppermute(pass_on, "core", [(0, 1), (1, 0)])
    group_mean = (half_sum + passed[256:, :128]).reshape(FEAT) / GROUP
    own_columns = lax.dynamic_slice_in_dim(got, 512 + 256 * core, 256, 2).reshape(256, 256)
    rows_mean = lax.dynamic_index_in_dim(group_mean.reshape(4, 4, 128), x, 1, False).reshape(512)
    centered_rows = (
        jnp.concatenate([got[:, :, :512].reshape(256, 512), passed[:256, :512]], 0) - rows_mean
    )
    centered_columns = jnp.concatenate([own_columns, passed[:256, 512:]], 0) - cut(
        group_mean, col_block, 256, 0
    )
    moments = jnp.einsum(
        "nf,nc->fc",
        centered_rows,
        centered_columns,
        precision=highest,
        preferred_element_type=jnp.float32,
    )
    parts = jnp.concatenate(
        [
            moments.reshape(4, 128, 256),
            jnp.broadcast_to(group_mean.reshape(1, 8, 256), (4, 8, 256)),
        ],
        axis=1,
    )
    parts = lax.all_to_all(parts, "y", 0, 0, tiled=True)
    means = parts[:, 128:].reshape(4, FEAT)
    feature_mean = jnp.sum(means, axis=0) / 4
    gap = means - feature_mean
    between = jnp.einsum(
        "gf,gc->fc",
        cut(gap, row_block, 128, 1),
        cut(gap, col_block, 256, 1),
        precision=highest,
        preferred_element_type=jnp.float32,
    )
    covariance = (jnp.sum(parts[:, :128], axis=0) + between * GROUP) / (IMAGES - 1)
    return feature_mean, covariance


def local(*arguments):
    return statistics(network(*arguments))


def solution(mesh):
    fine = Mesh(mesh.devices.reshape(4, 2, 2, 4, 2), AXES)
    placed = (P(AXES, None, None, None),) + (P(),) * 12
    return jax.shard_map(
        local,
        mesh=fine,
        in_specs=placed,
        out_specs=(P(), P(("y", "xh", "xl"), ("z", "core"))),
        check_vma=False,
    )
```

```python
import jax
import jax.numpy as jnp
from jax import lax
from jax.experimental import pallas as pl
from jax.experimental.pallas import tpu as pltpu
from jax.sharding import Mesh, PartitionSpec as P

AXES = ("y", "xh", "xl", "z", "core")
IMAGES = 2048
FEAT = 2048
LOCAL = 16
GROUP = 512


BF = jnp.bfloat16
F32 = jnp.float32


def relu(values):
    return jnp.maximum(values, 0.0).astype(BF)


def dot(a, b):
    return jnp.dot(a, b, preferred_element_type=F32)


def place_sum(values):
    return jnp.sum(values.astype(F32).reshape(64, LOCAL, -1), axis=0) * (1.0 / 64.0)


def network_kernel(
    x_hbm,
    entry_hbm,
    wide_hbm,
    row_hbm,
    column_hbm,
    reduce_hbm,
    second_hbm,
    second_row_hbm,
    second_column_hbm,
    second_deep_hbm,
    deep_row_hbm,
    deep_column_hbm,
    pool_hbm,
    out,
    x,
    entry_w,
    wide_w,
    row_w,
    column_w,
    reduce_w,
    second_w,
    second_row_w,
    second_column_w,
    second_deep_w,
    deep_row_w,
    deep_column_w,
    pool_w,
    row_pad,
    short,
    long,
    row_out,
    tower,
    middle,
    branch,
    deep,
    deep_out,
    averaged,
    features,
    sems,
):
    copies = {}

    def start(name, source, target, slot):
        copies[name] = pltpu.make_async_copy(source, target, sems.at[slot])
        copies[name].start()

    start("entry", entry_hbm, entry_w, 0)
    start("x0", x_hbm.at[pl.ds(0, 9)], x.at[pl.ds(0, 9)], 1)
    start("x1", x_hbm.at[pl.ds(9, 8)], x.at[pl.ds(9, 8)], 2)
    later = [
        ("row", row_hbm, row_w),
        ("column", column_hbm, column_w),
        ("wide", wide_hbm, wide_w),
        ("reduce", reduce_hbm, reduce_w),
        ("second", second_hbm, second_w),
        ("second_deep", second_deep_hbm, second_deep_w),
        ("second_row", second_row_hbm, second_row_w),
        ("second_column", second_column_hbm, second_column_w),
        ("deep_row", deep_row_hbm, deep_row_w),
        ("deep_column", deep_column_hbm, deep_column_w),
        ("pool", pool_hbm, pool_w),
    ]
    for i, (name, source, target) in enumerate(later):
        start(name, source, target, 3 + i)

    long[:, 0:3] = jnp.zeros((17, 3, LOCAL, 256), BF)
    long[:, 20:23] = jnp.zeros((17, 3, LOCAL, 256), BF)
    row_out[0:3] = jnp.zeros((3, 17, LOCAL, 192), BF)
    row_out[20:23] = jnp.zeros((3, 17, LOCAL, 192), BF)
    row_pad[:, 0:64] = jnp.zeros((7, 64, 192), BF)
    for array, channels in ((middle, 1280), (branch, 384), (deep, 448), (deep_out, 384)):
        array[0] = jnp.zeros((10, LOCAL, channels), BF)
        array[9] = jnp.zeros((10, LOCAL, channels), BF)
        array[1:9, 0] = jnp.zeros((8, LOCAL, channels), BF)
        array[1:9, 9] = jnp.zeros((8, LOCAL, channels), BF)

    copies["entry"].wait()
    copies["x0"].wait()

    def entry_block(i, carry):
        @pl.when(i == 1)
        def _():
            copies["x1"].wait()

        values = relu(dot(x[pl.ds(8 * i, 9)].reshape(2448, 768), entry_w[...]))
        values = values.reshape(9, 17, LOCAL, 384)
        long[pl.ds(8 * i, 9), 3:20] = values[..., 128:]
        for r in range(9):
            for c in range(17):
                short[r % 2, c % 2, 4 * i + r // 2, c // 2] = values[r, c, :, :192]
        return carry

    lax.fori_loop(0, 2, entry_block, 0)

    copies["row"].wait()
    row_pad[:, 64:] = row_w[...]

    def row_block(i, carry):
        values = sum(
            dot(long[pl.ds(8 * i, 9), t : t + 17].reshape(2448, 256), row_pad[t])
            for t in range(7)
        )
        row_out[pl.ds(8 * i + 3, 9)] = relu(values).reshape(9, 17, LOCAL, 192)
        for r in range(4):
            tall = jnp.maximum(
                jnp.maximum(x[8 * i + 2 * r], x[8 * i + 2 * r + 1]), x[8 * i + 2 * r + 2]
            )
            for c in range(8):
                middle[4 * i + r + 1, c + 1, :, 512:] = jnp.maximum(
                    jnp.maximum(tall[2 * c], tall[2 * c + 1]), tall[2 * c + 2]
                )
        return carry

    lax.fori_loop(0, 2, row_block, 0)
    copies["column"].wait()

    def column_block(i, carry):
        values = sum(
            dot(row_out[pl.ds(8 * i + t, 9)].reshape(2448, 192), column_w[t]) for t in range(7)
        )
        values = relu(values).reshape(9, 17, LOCAL, 192)
        for r in range(9):
            for c in range(17):
                tower[r % 2, c % 2, 4 * i + r // 2, c // 2] = values[r, c]
        return carry

    lax.fori_loop(0, 2, column_block, 0)
    copies["wide"].wait()
    copies["reduce"].wait()

    def strided(array, weights):
        return sum(
            dot(
                array[a % 2, b % 2, a // 2 : a // 2 + 8, b // 2 : b // 2 + 8].reshape(1024, 192),
                weights[a, b],
            )
            for a in range(3)
            for b in range(3)
        )

    wide_out = relu(strided(short, wide_w))
    middle[1:9, 1:9, :, 0:320] = wide_out.reshape(8, 8, LOCAL, 320)
    tower_out = relu(strided(tower, reduce_w))
    middle[1:9, 1:9, :, 320:512] = tower_out.reshape(8, 8, LOCAL, 192)

    copies["second"].wait()
    flat = middle[1:9, 1:9].reshape(1024, 1280)
    second = relu(dot(flat, second_w[...]))
    features[:, 0:320] = place_sum(second[:, 0:320])
    branch[1:9, 1:9] = second[:, 320:704].reshape(8, 8, LOCAL, 384)
    deep[1:9, 1:9] = second[:, 704:1152].reshape(8, 8, LOCAL, 448)

    def window(array, a, b):
        return array[a : a + 8, b : b + 8].reshape(1024, array.shape[3])

    def across(array, weights):
        taps = jnp.concatenate([window(array, 1, t) for t in range(3)], axis=1)
        return relu(dot(taps, weights[...].reshape(1152, 384)))

    def down(array, weights):
        taps = jnp.concatenate([window(array, t, 1) for t in range(3)], axis=1)
        return relu(dot(taps, weights[...].reshape(1152, 384)))

    copies["second_deep"].wait()
    deep_values = sum(
        dot(window(deep, a, b), second_deep_w[a, b]) for a in range(3) for b in range(3)
    )
    deep_out[1:9, 1:9] = relu(deep_values).reshape(8, 8, LOCAL, 384)

    for i in range(8):
        tall = (
            middle[i].astype(F32) + middle[i + 1].astype(F32) + middle[i + 2].astype(F32)
        )
        rows_inside = 3 - (i == 0) - (i == 7)
        for j in range(8):
            cells = rows_inside * (3 - (j == 0) - (j == 7))
            box = (tall[j] + tall[j + 1] + tall[j + 2]) * (1.0 / cells)
            averaged[i, j] = box.astype(BF)

    copies["second_row"].wait()
    features[:, 320:704] = place_sum(across(branch, second_row_w))
    copies["second_column"].wait()
    features[:, 704:1088] = place_sum(down(branch, second_column_w))
    copies["deep_row"].wait()
    features[:, 1088:1472] = place_sum(across(deep_out, deep_row_w))
    copies["deep_column"].wait()
    features[:, 1472:1856] = place_sum(down(deep_out, deep_column_w))
    copies["pool"].wait()
    pooled = lax.dot_general(
        averaged[...].reshape(1024, 1280),
        pool_w[...],
        (((1,), (1,)), ((), ())),
        preferred_element_type=F32,
    )
    features[:, 1856:2048] = place_sum(relu(pooled))

    for block in range(16):
        part = features[:, 128 * block : 128 * block + 128]
        total = jnp.sum(part, axis=0, keepdims=True)
        for target in range(16):
            target_x, target_z = target // 4, target % 4
            if block % 4 == target_x:
                out[target, :, 128 * (block // 4) : 128 * (block // 4) + 128] = part
            if block // 4 == target_z:
                out[target, :, 512 + 128 * (block % 4) : 640 + 128 * (block % 4)] = part
            out[target, block : block + 1, 1024:1152] = total


def network(
    block_inputs,
    first_entry,
    first_wide,
    first_row,
    first_column,
    first_reduce,
    second_entry,
    second_row,
    second_column,
    second_deep,
    deep_row,
    deep_column,
    pool_project,
):
    operands = (
        block_inputs.transpose(1, 2, 0, 3),
        first_entry[0, 0],
        first_wide,
        first_row[0],
        first_column[:, 0],
        first_reduce,
        second_entry[0, 0],
        second_row[0],
        second_column[:, 0],
        second_deep,
        deep_row[0],
        deep_column[:, 0],
        pool_project[0, 0].T,
    )
    place = lambda *shape: pltpu.VMEM(shape, BF)
    return pl.pallas_call(
        network_kernel,
        out_shape=jax.ShapeDtypeStruct((16, LOCAL, 1152), F32),
        in_specs=[pl.BlockSpec(memory_space=pl.ANY)] * 13,
        out_specs=pl.BlockSpec(memory_space=pltpu.VMEM),
        scratch_shapes=[pltpu.VMEM(a.shape, a.dtype) for a in operands]
        + [
            place(7, 256, 192),
            place(2, 2, 9, 9, LOCAL, 192),
            place(17, 23, LOCAL, 256),
            place(23, 17, LOCAL, 192),
            place(2, 2, 9, 9, LOCAL, 192),
            place(10, 10, LOCAL, 1280),
            place(10, 10, LOCAL, 384),
            place(10, 10, LOCAL, 448),
            place(10, 10, LOCAL, 384),
            place(8, 8, LOCAL, 1280),
            pltpu.VMEM((LOCAL, 2048), F32),
            pltpu.SemaphoreType.DMA((14,)),
        ],
        compiler_params=pltpu.CompilerParams(vmem_limit_bytes=67043328),
        cost_estimate=pl.CostEstimate(
            flops=19600000000, bytes_accessed=21000000, transcendentals=0
        ),
        name="network",
    )(*operands)


def cut(array, index, size, axis):
    return lax.dynamic_slice_in_dim(array, index * size, size, axis)


def statistics(message):
    highest = lax.Precision.HIGHEST
    x = lax.axis_index("xh") * 2 + lax.axis_index("xl")
    core = lax.axis_index("core")
    row_block = lax.axis_index("y") * 4 + x
    col_block = lax.axis_index("z") * 2 + core
    got = lax.all_to_all(message, ("xh", "xl", "z"), 0, 0, tiled=True)
    half_sum = jnp.sum(got[:, :, 1024:], axis=0)
    other_columns = lax.dynamic_slice_in_dim(got, 512 + 256 * (1 - core), 256, 2)
    pass_on = jnp.concatenate([got[:, :, :512], other_columns], -1).reshape(256, 768)
    pass_on = jnp.concatenate(
        [pass_on, jnp.pad(half_sum, ((0, 0), (0, 640)))], 0
    )
    passed = lax.ppermute(pass_on, "core", [(0, 1), (1, 0)])
    group_mean = (half_sum + passed[256:, :128]).reshape(FEAT) / GROUP
    own_columns = lax.dynamic_slice_in_dim(got, 512 + 256 * core, 256, 2).reshape(256, 256)
    rows_mean = lax.dynamic_index_in_dim(group_mean.reshape(4, 4, 128), x, 1, False).reshape(512)
    centered_rows = (
        jnp.concatenate([got[:, :, :512].reshape(256, 512), passed[:256, :512]], 0) - rows_mean
    )
    centered_columns = jnp.concatenate([own_columns, passed[:256, 512:]], 0) - cut(
        group_mean, col_block, 256, 0
    )
    moments = jnp.einsum(
        "nf,nc->fc",
        centered_rows,
        centered_columns,
        precision=highest,
        preferred_element_type=jnp.float32,
    )
    parts = jnp.concatenate(
        [
            moments.reshape(4, 128, 256),
            jnp.broadcast_to(group_mean.reshape(1, 8, 256), (4, 8, 256)),
        ],
        axis=1,
    )
    parts = lax.all_to_all(parts, "y", 0, 0, tiled=True)
    means = parts[:, 128:].reshape(4, FEAT)
    feature_mean = jnp.sum(means, axis=0) / 4
    gap = means - feature_mean
    between = jnp.einsum(
        "gf,gc->fc",
        cut(gap, row_block, 128, 1),
        cut(gap, col_block, 256, 1),
        precision=highest,
        preferred_element_type=jnp.float32,
    )
    covariance = (jnp.sum(parts[:, :128], axis=0) + between * GROUP) / (IMAGES - 1)
    return feature_mean, covariance


def local(*arguments):
    return statistics(network(*arguments))


def solution(mesh):
    fine = Mesh(mesh.devices.reshape(4, 2, 2, 4, 2), AXES)
    placed = (P(AXES, None, None, None),) + (P(),) * 12
    return jax.shard_map(
        local,
        mesh=fine,
        in_specs=placed,
        out_specs=(P(), P(("y", "xh", "xl"), ("z", "core"))),
        check_vma=False,
    )
```

```python
import functools

import jax
import jax.numpy as jnp
from jax import lax
from jax.experimental import pallas as pl
from jax.experimental.pallas import tpu as pltpu
from jax.sharding import Mesh, PartitionSpec as P

AXES = ("y", "xh", "xl", "z", "core")
IMAGES = 2048
FEAT = 2048
LOCAL = 16
GROUP = 512


BF = jnp.bfloat16
F32 = jnp.float32


def relu(values):
    return jnp.maximum(values, 0.0).astype(BF)


def dot(a, b):
    return jnp.dot(a, b, preferred_element_type=F32)


def pack(taps, head, joint, tail):
    tiles = []

    def split(values):
        tiles.extend(values[:, c : c + 128] for c in range(0, values.shape[1], 128))

    for t in range(0, taps - 1, 2):
        split(head(t))
        tiles.append(joint(t, t + 1))
        split(tail(t + 1))
    split(head(taps - 1))
    tiles.append(joint(taps - 1, taps - 1)[:, :64])
    return tiles


def contract(tiles, weights, fillers=(), step=4):
    values, row = None, 0
    groups = range(0, len(tiles), step)
    for n, first in enumerate(groups):
        part = jnp.concatenate(tiles[first : first + step], axis=1)
        product = dot(part, weights[row : row + part.shape[1]])
        row += part.shape[1]
        values = product if values is None else values + product
        for filler in fillers[len(fillers) * n // len(groups) : len(fillers) * (n + 1) // len(groups)]:
            filler()
    return values


def network_kernel(
    x_hbm,
    entry_hbm,
    wide_hbm,
    row_hbm,
    column_hbm,
    reduce_hbm,
    second_hbm,
    second_row_hbm,
    second_column_hbm,
    second_deep_hbm,
    deep_row_hbm,
    deep_column_hbm,
    pool_hbm,
    out,
    x,
    entry_w,
    wide_w,
    row_w,
    column_w,
    reduce_w,
    second_w,
    second_deep_w,
    branch_w,
    pool_w,
    long_head,
    long_joint,
    long_tail,
    row_head,
    row_joint,
    row_tail,
    short_head,
    short_ends,
    short_tail,
    tower_head,
    tower_ends,
    tower_tail,
    middle,
    branch,
    deep_head,
    deep_last,
    deep_first,
    deep_tail,
    averaged,
    branch_sums,
    features,
    sems,
):
    copies = {}

    def start(name, source, target, slot):
        copies[name] = pltpu.make_async_copy(source, target, sems.at[slot])
        copies[name].start()

    start("entry", entry_hbm, entry_w, 0)
    start("x0", x_hbm.at[pl.ds(0, 9)], x.at[pl.ds(0, 9)], 1)
    start("x1", x_hbm.at[pl.ds(9, 8)], x.at[pl.ds(9, 8)], 2)
    later = [
        ("row", row_hbm, row_w),
        ("column", column_hbm, column_w),
        ("wide", wide_hbm, wide_w),
        ("reduce", reduce_hbm, reduce_w),
        ("second", second_hbm, second_w),
        ("second_deep", second_deep_hbm, second_deep_w),
        ("second_row", second_row_hbm, branch_w.at[0]),
        ("second_column", second_column_hbm, branch_w.at[1]),
        ("deep_row", deep_row_hbm, branch_w.at[2]),
        ("deep_column", deep_column_hbm, branch_w.at[3]),
        ("pool", pool_hbm, pool_w),
    ]
    for i, (name, source, target) in enumerate(later):
        start(name, source, target, 3 + i)

    deep_last[...] = jnp.zeros((10, 10, LOCAL, 128), BF)
    deep_first[...] = jnp.zeros((10, 10, LOCAL, 128), BF)
    for array in (long_head, long_joint, long_tail):
        array[:, 0:3] = jnp.zeros((17, 3, LOCAL, 128), BF)
        array[:, 19:23] = jnp.zeros((17, 4, LOCAL, 128), BF)
    for array in (row_head, row_joint, row_tail):
        array[0:3] = jnp.zeros((3, 17, LOCAL, 128), BF)
        array[19:23] = jnp.zeros((4, 17, LOCAL, 128), BF)
    margins = [(middle, 1280), (deep_head, 384), (deep_tail, 384)]
    for array, channels in margins + [(branch.at[0], 384), (branch.at[1], 384)]:
        array[0] = jnp.zeros((10, LOCAL, channels), BF)
        array[9] = jnp.zeros((10, LOCAL, channels), BF)
        array[1:9, 0] = jnp.zeros((8, LOCAL, channels), BF)
        array[1:9, 9] = jnp.zeros((8, LOCAL, channels), BF)

    def split_by_parity(i, first, values, head, ends, tail):
        for r in range(first, first + 3):
            for c in range(17):
                at = (r % 2, c % 2, 4 * i + r // 2, c // 2)
                place = values[r - first, c]
                head[at] = place[:, 0:128]
                ends[(*at, slice(None), slice(0, 64))] = place[:, 128:192]
                ends[(*at, slice(None), slice(64, 128))] = place[:, 0:64]
                tail[at] = place[:, 64:192]

    def in_thirds(product, keep):
        earlier = product(0)
        for first in (3, 6):
            latter = product(first)
            keep(first - 3, earlier)
            earlier = latter
        keep(6, earlier)

    copies["entry"].wait()
    copies["x0"].wait()

    def entry_block(i, carry):
        @pl.when(i == 1)
        def _():
            copies["x1"].wait()

        def product(first):
            return dot(x[pl.ds(8 * i + first, 3)].reshape(816, 768), entry_w[...])

        def keep(first, values):
            values = relu(values).reshape(3, 17, LOCAL, 384)
            rows = pl.ds(8 * i + first, 3)
            long_head[rows, 3:20] = values[..., 192:320]
            long_joint[rows, 3:20, :, 0:64] = values[..., 320:384]
            long_joint[rows, 2:19, :, 64:128] = values[..., 192:256]
            long_tail[rows, 3:20] = values[..., 256:384]
            split_by_parity(i, first, values, short_head, short_ends, short_tail)

        in_thirds(product, keep)
        return carry

    lax.fori_loop(0, 2, entry_block, 0)

    copies["row"].wait()

    def maximum(i, r):
        tall = [
            jnp.maximum(
                jnp.maximum(x[8 * i + 2 * r, c], x[8 * i + 2 * r + 1, c]), x[8 * i + 2 * r + 2, c]
            )
            for c in range(17)
        ]
        for c in range(8):
            middle[4 * i + r + 1, c + 1, :, 512:] = jnp.maximum(
                jnp.maximum(tall[2 * c], tall[2 * c + 1]), tall[2 * c + 2]
            )

    def row_block(i, carry):
        def at(array, t):
            return array[pl.ds(8 * i, 9), t : t + 17].reshape(2448, 128)

        tiles = pack(
            7,
            lambda t: at(long_head, t),
            lambda t, u: at(long_joint, t),
            lambda t: at(long_tail, t),
        )
        fillers = [functools.partial(maximum, i, r) for r in range(4)]
        values = relu(contract(tiles, row_w, fillers)).reshape(9, 17, LOCAL, 192)
        row_head[pl.ds(8 * i + 3, 9)] = values[..., 0:128]
        row_joint[pl.ds(8 * i + 3, 9), :, :, 0:64] = values[..., 128:192]
        row_joint[pl.ds(8 * i + 2, 9), :, :, 64:128] = values[..., 0:64]
        row_tail[pl.ds(8 * i + 3, 9)] = values[..., 64:192]
        return carry

    lax.fori_loop(0, 2, row_block, 0)
    copies["column"].wait()

    def column_block(i, carry):
        def at(array, t):
            return array[pl.ds(8 * i + t, 9)].reshape(2448, 128)

        tiles = pack(
            7,
            lambda t: at(row_head, t),
            lambda t, u: at(row_joint, t),
            lambda t: at(row_tail, t),
        )
        values = relu(contract(tiles, column_w)).reshape(9, 17, LOCAL, 192)
        for first in (0, 3, 6):
            split_by_parity(
                i, first, values[first : first + 3], tower_head, tower_ends, tower_tail
            )
        return carry

    lax.fori_loop(0, 2, column_block, 0)
    copies["wide"].wait()
    copies["reduce"].wait()

    def half_map(step):
        lax.fori_loop(0, 2, lambda i, carry: step(4 * i), None)

    lower = lax.broadcasted_iota(jnp.int32, (512, 128), 1) < 64

    def joined(ends, t, u):
        return jnp.where(lower, ends(t), ends(u))

    def strided(arrays, weights, i):
        def at(array, t):
            a, b = t // 3, t % 3
            window = array[a % 2, b % 2, pl.ds(i + a // 2, 4), b // 2 : b // 2 + 8]
            return window.reshape(512, 128)

        head, ends, tail = (functools.partial(at, array) for array in arrays)
        return relu(contract(pack(9, head, functools.partial(joined, ends), tail), weights))

    def reduce_block(i):
        wide_out = strided((short_head, short_ends, short_tail), wide_w, i)
        middle[pl.ds(i + 1, 4), 1:9, :, 0:320] = wide_out.reshape(4, 8, LOCAL, 320)
        tower_out = strided((tower_head, tower_ends, tower_tail), reduce_w, i)
        middle[pl.ds(i + 1, 4), 1:9, :, 320:512] = tower_out.reshape(4, 8, LOCAL, 192)

    half_map(reduce_block)

    def add_sums(i, first, values):
        part = jnp.sum(values.astype(F32).reshape(32, LOCAL, -1), axis=0)
        at = slice(first, first + part.shape[1])
        features[:, at] = jnp.where(i == 0, 0.0, features[:, at]) + part

    copies["second"].wait()

    def second_block(i):
        flat = middle[pl.ds(i + 1, 4), 1:9].reshape(512, 1280)
        second = relu(dot(flat, second_w[...]))
        add_sums(i, 0, second[:, 0:320])
        rows = pl.ds(i + 1, 4)
        branch[0, rows, 1:9] = second[:, 320:704].reshape(4, 8, LOCAL, 384)
        deep_head[rows, 1:9] = second[:, 704:1088].reshape(4, 8, LOCAL, 384)
        deep_last[rows, 1:9, :, 0:64] = second[:, 1088:1152].reshape(4, 8, LOCAL, 64)
        deep_first[rows, 1:9, :, 64:128] = second[:, 704:768].reshape(4, 8, LOCAL, 64)
        deep_tail[rows, 1:9] = second[:, 768:1152].reshape(4, 8, LOCAL, 384)

    half_map(second_block)

    copies["second_deep"].wait()

    def average(i, r, first):
        at = slice(first, first + 256)
        edge = i + r == (0 if r < 2 else 7)
        columns = [
            middle[i + r, j, :, at].astype(F32)
            + middle[i + r + 1, j, :, at].astype(F32)
            + middle[i + r + 2, j, :, at].astype(F32)
            for j in range(10)
        ]
        for j in range(8):
            width = 3 - (j == 0) - (j == 7)
            scale = jnp.where(edge, 1.0 / (2 * width), 1.0 / (3 * width))
            box = (columns[j] + columns[j + 1] + columns[j + 2]) * scale
            averaged[i + r, j, :, at] = box.astype(BF)

    def deep_block(i):
        def at(array, t):
            window = array[pl.ds(i + t // 3, 4), t % 3 : t % 3 + 8]
            return window.reshape(512, array.shape[3])

        tiles = pack(
            9,
            lambda t: at(deep_head, t),
            lambda t, u: at(deep_last, t) + at(deep_first, u),
            lambda t: at(deep_tail, t),
        )
        fillers = [functools.partial(average, i, r, 256 * n) for n in range(5) for r in range(4)]
        values = relu(contract(tiles, second_deep_w, fillers))
        branch[1, pl.ds(i + 1, 4), 1:9] = values.reshape(4, 8, LOCAL, 384)

    half_map(deep_block)
    for name in ("second_row", "second_column", "deep_row", "deep_column"):
        copies[name].wait()

    def branch_map(n, carry):
        def tap(t):
            down, right = jnp.where(n % 2 == 0, 1, t), jnp.where(n % 2 == 0, t, 1)
            return branch[n // 2, pl.ds(down, 8), pl.ds(right, 8)].reshape(1024, 384)

        values = relu(dot(jnp.concatenate([tap(t) for t in range(3)], axis=1), branch_w[n]))
        branch_sums[n] = jnp.sum(values.astype(F32).reshape(64, LOCAL, 384), axis=0)
        return carry

    lax.fori_loop(0, 4, branch_map, 0)
    for n in range(4):
        features[:, 320 + 384 * n : 704 + 384 * n] = branch_sums[n]
    copies["pool"].wait()

    def pool_block(i):
        pooled = lax.dot_general(
            averaged[pl.ds(i, 4)].reshape(512, 1280),
            pool_w[...],
            (((1,), (1,)), ((), ())),
            preferred_element_type=F32,
        )
        add_sums(i, 1856, relu(pooled))

    half_map(pool_block)

    for block in range(16):
        part = features[:, 128 * block : 128 * block + 128] * (1.0 / 64.0)
        total = jnp.sum(part, axis=0, keepdims=True)
        for target in range(16):
            target_x, target_z = target // 4, target % 4
            if block % 4 == target_x:
                out[target, :, 128 * (block // 4) : 128 * (block // 4) + 128] = part
            if block // 4 == target_z:
                out[target, :, 512 + 128 * (block % 4) : 640 + 128 * (block % 4)] = part
            out[target, block : block + 1, 1024:1152] = total


def network(
    block_inputs,
    first_entry,
    first_wide,
    first_row,
    first_column,
    first_reduce,
    second_entry,
    second_row,
    second_column,
    second_deep,
    deep_row,
    deep_column,
    pool_project,
):
    operands = (
        block_inputs.transpose(1, 2, 0, 3),
        first_entry[0, 0],
        first_wide.reshape(1728, 320),
        first_row.reshape(1344, 192),
        first_column.reshape(1344, 192),
        first_reduce.reshape(1728, 192),
        second_entry[0, 0],
        second_row.reshape(1152, 384),
        second_column.reshape(1152, 384),
        second_deep.reshape(4032, 384),
        deep_row.reshape(1152, 384),
        deep_column.reshape(1152, 384),
        pool_project[0, 0].T,
    )
    place = lambda *shape: pltpu.VMEM(shape, BF)
    return pl.pallas_call(
        network_kernel,
        out_shape=jax.ShapeDtypeStruct((16, LOCAL, 1152), F32),
        in_specs=[pl.BlockSpec(memory_space=pl.ANY)] * 13,
        out_specs=pl.BlockSpec(memory_space=pltpu.VMEM),
        scratch_shapes=[place(*a.shape) for a in operands[:7]]
        + [place(4032, 384), place(4, 1152, 384), place(192, 1280)]
        + [place(17, 23, LOCAL, 128)] * 3
        + [place(23, 17, LOCAL, 128)] * 3
        + [place(2, 2, 9, 9, LOCAL, 128)] * 6
        + [
            place(10, 10, LOCAL, 1280),
            place(2, 10, 10, LOCAL, 384),
            place(10, 10, LOCAL, 384),
            place(10, 10, LOCAL, 128),
            place(10, 10, LOCAL, 128),
            place(10, 10, LOCAL, 384),
            place(8, 8, LOCAL, 1280),
            pltpu.VMEM((4, LOCAL, 384), F32),
            pltpu.VMEM((LOCAL, 2048), F32),
            pltpu.SemaphoreType.DMA((14,)),
        ],
        compiler_params=pltpu.CompilerParams(vmem_limit_bytes=67043328),
        cost_estimate=pl.CostEstimate(
            flops=19600000000, bytes_accessed=21000000, transcendentals=0
        ),
        name="network",
    )(*operands)


def cut(array, index, size, axis):
    return lax.dynamic_slice_in_dim(array, index * size, size, axis)


def statistics(message):
    highest = lax.Precision.HIGHEST
    x = lax.axis_index("xh") * 2 + lax.axis_index("xl")
    core = lax.axis_index("core")
    row_block = lax.axis_index("y") * 4 + x
    col_block = lax.axis_index("z") * 2 + core
    got = lax.all_to_all(message, ("xh", "xl", "z"), 0, 0, tiled=True)
    half_sum = jnp.sum(got[:, :, 1024:], axis=0)
    other_columns = lax.dynamic_slice_in_dim(got, 512 + 256 * (1 - core), 256, 2)
    pass_on = jnp.concatenate([got[:, :, :512], other_columns], -1).reshape(256, 768)
    pass_on = jnp.concatenate(
        [pass_on, jnp.pad(half_sum, ((0, 0), (0, 640)))], 0
    )
    passed = lax.ppermute(pass_on, "core", [(0, 1), (1, 0)])
    group_mean = (half_sum + passed[256:, :128]).reshape(FEAT) / GROUP
    own_columns = lax.dynamic_slice_in_dim(got, 512 + 256 * core, 256, 2).reshape(256, 256)
    rows_mean = lax.dynamic_index_in_dim(group_mean.reshape(4, 4, 128), x, 1, False).reshape(512)
    centered_rows = (
        jnp.concatenate([got[:, :, :512].reshape(256, 512), passed[:256, :512]], 0) - rows_mean
    )
    centered_columns = jnp.concatenate([own_columns, passed[:256, 512:]], 0) - cut(
        group_mean, col_block, 256, 0
    )
    moments = jnp.einsum(
        "nf,nc->fc",
        centered_rows,
        centered_columns,
        precision=highest,
        preferred_element_type=jnp.float32,
    )
    parts = jnp.concatenate(
        [
            moments.reshape(4, 128, 256),
            jnp.broadcast_to(group_mean.reshape(1, 8, 256), (4, 8, 256)),
        ],
        axis=1,
    )
    parts = lax.all_to_all(parts, "y", 0, 0, tiled=True)
    means = parts[:, 128:].reshape(4, FEAT)
    feature_mean = jnp.sum(means, axis=0) / 4
    gap = means - feature_mean
    between = jnp.einsum(
        "gf,gc->fc",
        cut(gap, row_block, 128, 1),
        cut(gap, col_block, 256, 1),
        precision=highest,
        preferred_element_type=jnp.float32,
    )
    covariance = (jnp.sum(parts[:, :128], axis=0) + between * GROUP) / (IMAGES - 1)
    return feature_mean, covariance


def local(*arguments):
    return statistics(network(*arguments))


def solution(mesh):
    fine = Mesh(mesh.devices.reshape(4, 2, 2, 4, 2), AXES)
    placed = (P(AXES, None, None, None),) + (P(),) * 12
    return jax.shard_map(
        local,
        mesh=fine,
        in_specs=placed,
        out_specs=(P(), P(("y", "xh", "xl"), ("z", "core"))),
        check_vma=False,
    )
```

```python
import functools

import jax
import jax.numpy as jnp
from jax import lax
from jax.experimental import pallas as pl
from jax.experimental.pallas import tpu as pltpu
from jax.sharding import Mesh, PartitionSpec as P

AXES = ("y", "xh", "xl", "z", "core")
IMAGES = 2048
FEAT = 2048
LOCAL = 16
GROUP = 512


BF = jnp.bfloat16
F32 = jnp.float32


def relu(values):
    return jnp.maximum(values, 0.0).astype(BF)


def dot(a, b):
    return jnp.dot(a, b, preferred_element_type=F32)


def pack(taps, head, joint, tail):
    tiles = []

    def split(values):
        tiles.extend(values[:, c : c + 128] for c in range(0, values.shape[1], 128))

    for t in range(0, taps - 1, 2):
        split(head(t))
        tiles.append(joint(t, t + 1))
        split(tail(t + 1))
    split(head(taps - 1))
    tiles.append(joint(taps - 1, taps - 1)[:, :64])
    return tiles


def contract(tiles, weights, fillers=(), step=4):
    values, row = None, 0
    groups = range(0, len(tiles), step)
    for n, first in enumerate(groups):
        part = jnp.concatenate(tiles[first : first + step], axis=1)
        product = dot(part, weights[row : row + part.shape[1]])
        row += part.shape[1]
        values = product if values is None else values + product
        for filler in fillers[len(fillers) * n // len(groups) : len(fillers) * (n + 1) // len(groups)]:
            filler()
    return values


def network_kernel(
    x_hbm,
    entry_hbm,
    wide_hbm,
    row_hbm,
    column_hbm,
    reduce_hbm,
    second_hbm,
    second_row_hbm,
    second_column_hbm,
    second_deep_hbm,
    deep_row_hbm,
    deep_column_hbm,
    pool_hbm,
    out,
    x,
    entry_w,
    wide_w,
    row_w,
    column_w,
    reduce_w,
    second_w,
    second_deep_w,
    branch_w,
    pool_w,
    long_head,
    long_joint,
    long_tail,
    row_head,
    row_joint,
    row_tail,
    short_head,
    short_ends,
    short_tail,
    tower_head,
    tower_ends,
    tower_tail,
    middle,
    branch,
    deep_head,
    deep_last,
    deep_first,
    deep_tail,
    averaged,
    branch_sums,
    features,
    sems,
):
    def copy(name):
        source, target, slot = moves[name]
        return pltpu.make_async_copy(source, target, sems.at[slot])

    moves = {"entry": (entry_hbm, entry_w, 0)}
    copy("entry").start()
    def x_third(i, first):
        source = x_hbm.at[pl.ds(8 * i + first, 3)]
        target = x.at[pl.ds(9 * i + first, 3)]
        return pltpu.make_async_copy(source, target, sems.at[1 + 3 * i + first // 3])

    for i in range(2):
        for first in (0, 3, 6):
            x_third(i, first).start()

    def start_later():
        for name, _, _ in later:
            copy(name).start()

    later = [
        ("row", row_hbm, row_w),
        ("column", column_hbm, column_w),
        ("wide", wide_hbm, wide_w),
        ("reduce", reduce_hbm, reduce_w),
        ("second", second_hbm, second_w),
        ("second_deep", second_deep_hbm, second_deep_w),
        ("second_row", second_row_hbm, branch_w.at[0]),
        ("second_column", second_column_hbm, branch_w.at[1]),
        ("deep_row", deep_row_hbm, branch_w.at[2]),
        ("deep_column", deep_column_hbm, branch_w.at[3]),
        ("pool", pool_hbm, pool_w),
    ]
    for i, (name, source, target) in enumerate(later):
        moves[name] = (source, target, 7 + i)

    deep_last[...] = jnp.zeros((10, 10, LOCAL, 128), BF)
    deep_first[...] = jnp.zeros((10, 10, LOCAL, 128), BF)
    for array in (long_head, long_joint, long_tail):
        array[:, 0:3] = jnp.zeros((17, 3, LOCAL, 128), BF)
        array[:, 19:23] = jnp.zeros((17, 4, LOCAL, 128), BF)
    for array in (row_head, row_joint, row_tail):
        array[0:3] = jnp.zeros((3, 17, LOCAL, 128), BF)
        array[19:23] = jnp.zeros((4, 17, LOCAL, 128), BF)
    margins = [(middle, 1280), (deep_head, 384), (deep_tail, 384)]
    for array, channels in margins + [(branch.at[0], 384), (branch.at[1], 384)]:
        array[0] = jnp.zeros((10, LOCAL, channels), BF)
        array[9] = jnp.zeros((10, LOCAL, channels), BF)
        array[1:9, 0] = jnp.zeros((8, LOCAL, channels), BF)
        array[1:9, 9] = jnp.zeros((8, LOCAL, channels), BF)

    def split_by_parity(i, first, values, head, ends, tail):
        for r in range(first, first + 3):
            for c in range(17):
                at = (r % 2, c % 2, 4 * i + r // 2, c // 2)
                place = values[r - first, c]
                head[at] = place[:, 0:128]
                ends[(*at, slice(None), slice(0, 64))] = place[:, 128:192]
                ends[(*at, slice(None), slice(64, 128))] = place[:, 0:64]
                tail[at] = place[:, 64:192]

    def in_thirds(product, keep):
        earlier = product(0)
        for first in (3, 6):
            latter = product(first)
            keep(first - 3, earlier)
            earlier = latter
        keep(6, earlier)

    copy("entry").wait()

    def entry_block(i, carry):
        @pl.when(i == 1)
        def _():
            start_later()

        def product(first):
            x_third(i, first).wait()
            return dot(x[pl.ds(9 * i + first, 3)].reshape(816, 768), entry_w[...])

        def keep(first, values):
            values = relu(values).reshape(3, 17, LOCAL, 384)
            rows = pl.ds(8 * i + first, 3)
            long_head[rows, 3:20] = values[..., 192:320]
            long_joint[rows, 3:20, :, 0:64] = values[..., 320:384]
            long_joint[rows, 2:19, :, 64:128] = values[..., 192:256]
            long_tail[rows, 3:20] = values[..., 256:384]
            split_by_parity(i, first, values, short_head, short_ends, short_tail)

        in_thirds(product, keep)
        return carry

    lax.fori_loop(0, 2, entry_block, 0)

    copy("row").wait()

    def maximum(i, r):
        tall = [
            jnp.maximum(
                jnp.maximum(x[9 * i + 2 * r, c], x[9 * i + 2 * r + 1, c]), x[9 * i + 2 * r + 2, c]
            )
            for c in range(17)
        ]
        for c in range(8):
            middle[4 * i + r + 1, c + 1, :, 512:] = jnp.maximum(
                jnp.maximum(tall[2 * c], tall[2 * c + 1]), tall[2 * c + 2]
            )

    def row_block(i, carry):
        def at(array, t):
            return array[pl.ds(8 * i, 9), t : t + 17].reshape(2448, 128)

        tiles = pack(
            7,
            lambda t: at(long_head, t),
            lambda t, u: at(long_joint, t),
            lambda t: at(long_tail, t),
        )
        fillers = [functools.partial(maximum, i, r) for r in range(4)]
        values = relu(contract(tiles, row_w, fillers)).reshape(9, 17, LOCAL, 192)
        row_head[pl.ds(8 * i + 3, 9)] = values[..., 0:128]
        row_joint[pl.ds(8 * i + 3, 9), :, :, 0:64] = values[..., 128:192]
        row_joint[pl.ds(8 * i + 2, 9), :, :, 64:128] = values[..., 0:64]
        row_tail[pl.ds(8 * i + 3, 9)] = values[..., 64:192]
        return carry

    lax.fori_loop(0, 2, row_block, 0)
    copy("column").wait()

    def column_block(i, carry):
        def at(array, t):
            return array[pl.ds(8 * i + t, 9)].reshape(2448, 128)

        tiles = pack(
            7,
            lambda t: at(row_head, t),
            lambda t, u: at(row_joint, t),
            lambda t: at(row_tail, t),
        )
        values = relu(contract(tiles, column_w)).reshape(9, 17, LOCAL, 192)
        for first in (0, 3, 6):
            split_by_parity(
                i, first, values[first : first + 3], tower_head, tower_ends, tower_tail
            )
        return carry

    lax.fori_loop(0, 2, column_block, 0)
    copy("wide").wait()
    copy("reduce").wait()

    def half_map(step):
        lax.fori_loop(0, 2, lambda i, carry: step(4 * i), None)

    lower = lax.broadcasted_iota(jnp.int32, (512, 128), 1) < 64

    def joined(ends, t, u):
        return jnp.where(lower, ends(t), ends(u))

    def strided(arrays, weights, i):
        def at(array, t):
            a, b = t // 3, t % 3
            window = array[a % 2, b % 2, pl.ds(i + a // 2, 4), b // 2 : b // 2 + 8]
            return window.reshape(512, 128)

        head, ends, tail = (functools.partial(at, array) for array in arrays)
        return relu(contract(pack(9, head, functools.partial(joined, ends), tail), weights))

    def reduce_block(i):
        wide_out = strided((short_head, short_ends, short_tail), wide_w, i)
        middle[pl.ds(i + 1, 4), 1:9, :, 0:320] = wide_out.reshape(4, 8, LOCAL, 320)
        tower_out = strided((tower_head, tower_ends, tower_tail), reduce_w, i)
        middle[pl.ds(i + 1, 4), 1:9, :, 320:512] = tower_out.reshape(4, 8, LOCAL, 192)

    half_map(reduce_block)

    def add_sums(i, first, values):
        part = jnp.sum(values.astype(F32).reshape(32, LOCAL, -1), axis=0)
        at = slice(first, first + part.shape[1])
        features[:, at] = jnp.where(i == 0, 0.0, features[:, at]) + part

    copy("second").wait()

    def second_block(i):
        flat = middle[pl.ds(i + 1, 4), 1:9].reshape(512, 1280)
        second = relu(dot(flat, second_w[...]))
        add_sums(i, 0, second[:, 0:320])
        rows = pl.ds(i + 1, 4)
        branch[0, rows, 1:9] = second[:, 320:704].reshape(4, 8, LOCAL, 384)
        deep_head[rows, 1:9] = second[:, 704:1088].reshape(4, 8, LOCAL, 384)
        deep_last[rows, 1:9, :, 0:64] = second[:, 1088:1152].reshape(4, 8, LOCAL, 64)
        deep_first[rows, 1:9, :, 64:128] = second[:, 704:768].reshape(4, 8, LOCAL, 64)
        deep_tail[rows, 1:9] = second[:, 768:1152].reshape(4, 8, LOCAL, 384)

    half_map(second_block)

    copy("second_deep").wait()
    copy("pool").wait()

    def average(i, r, first):
        at = slice(first, first + 256)
        edge = i + r == (0 if r < 2 else 7)
        columns = [
            middle[i + r, j, :, at].astype(F32)
            + middle[i + r + 1, j, :, at].astype(F32)
            + middle[i + r + 2, j, :, at].astype(F32)
            for j in range(10)
        ]
        for j in range(8):
            width = 3 - (j == 0) - (j == 7)
            scale = jnp.where(edge, 1.0 / (2 * width), 1.0 / (3 * width))
            box = (columns[j] + columns[j + 1] + columns[j + 2]) * scale
            averaged[i + r, j, :, at] = box.astype(BF)

    def deep_block(i):
        def at(array, t):
            window = array[pl.ds(i + t // 3, 4), t % 3 : t % 3 + 8]
            return window.reshape(512, array.shape[3])

        tiles = pack(
            9,
            lambda t: at(deep_head, t),
            lambda t, u: at(deep_last, t) + at(deep_first, u),
            lambda t: at(deep_tail, t),
        )
        fillers = [functools.partial(average, i, r, 256 * n) for n in range(5) for r in range(4)]
        values = relu(contract(tiles, second_deep_w, fillers, 8))
        branch[1, pl.ds(i + 1, 4), 1:9] = values.reshape(4, 8, LOCAL, 384)
        pooled = lax.dot_general(
            averaged[pl.ds(i, 4)].reshape(512, 1280),
            pool_w[...],
            (((1,), (1,)), ((), ())),
            preferred_element_type=F32,
        )
        add_sums(i, 1856, relu(pooled))

    half_map(deep_block)
    for name in ("second_row", "second_column", "deep_row", "deep_column"):
        copy(name).wait()

    def branch_map(n, carry):
        def tap(t):
            down, right = jnp.where(n % 2 == 0, 1, t), jnp.where(n % 2 == 0, t, 1)
            return branch[n // 2, pl.ds(down, 8), pl.ds(right, 8)].reshape(1024, 384)

        values = relu(dot(jnp.concatenate([tap(t) for t in range(3)], axis=1), branch_w[n]))
        branch_sums[n] = jnp.sum(values.astype(F32).reshape(64, LOCAL, 384), axis=0)
        return carry

    lax.fori_loop(0, 4, branch_map, 0)
    for n in range(4):
        features[:, 320 + 384 * n : 704 + 384 * n] = branch_sums[n]
    for block in range(16):
        part = features[:, 128 * block : 128 * block + 128] * (1.0 / 64.0)
        total = jnp.sum(part, axis=0, keepdims=True)
        own_y, own_x = block // 4, block % 4
        for target in range(16):
            target_x, target_z = target // 4, target % 4
            slot = None
            if own_y == target_z:
                slot = own_x
            elif own_x == target_x:
                slot = 4 + own_y - (own_y > target_z)
            if slot is not None:
                out[target, :, 128 * slot : 128 * slot + 128] = part
            out[target, block : block + 1, 896:1024] = total


def network(
    block_inputs,
    first_entry,
    first_wide,
    first_row,
    first_column,
    first_reduce,
    second_entry,
    second_row,
    second_column,
    second_deep,
    deep_row,
    deep_column,
    pool_project,
):
    operands = (
        block_inputs.transpose(1, 2, 0, 3),
        first_entry[0, 0],
        first_wide.reshape(1728, 320),
        first_row.reshape(1344, 192),
        first_column.reshape(1344, 192),
        first_reduce.reshape(1728, 192),
        second_entry[0, 0],
        second_row.reshape(1152, 384),
        second_column.reshape(1152, 384),
        second_deep.reshape(4032, 384),
        deep_row.reshape(1152, 384),
        deep_column.reshape(1152, 384),
        pool_project[0, 0].T,
    )
    place = lambda *shape: pltpu.VMEM(shape, BF)
    return pl.pallas_call(
        network_kernel,
        out_shape=jax.ShapeDtypeStruct((16, LOCAL, 1024), F32),
        in_specs=[pl.BlockSpec(memory_space=pl.ANY)] * 13,
        out_specs=pl.BlockSpec(memory_space=pltpu.VMEM),
        scratch_shapes=[place(18, 17, LOCAL, 768)]
        + [place(*a.shape) for a in operands[1:7]]
        + [place(4032, 384), place(4, 1152, 384), place(192, 1280)]
        + [place(17, 23, LOCAL, 128)] * 3
        + [place(23, 17, LOCAL, 128)] * 3
        + [place(2, 2, 9, 9, LOCAL, 128)] * 6
        + [
            place(10, 10, LOCAL, 1280),
            place(2, 10, 10, LOCAL, 384),
            place(10, 10, LOCAL, 384),
            place(10, 10, LOCAL, 128),
            place(10, 10, LOCAL, 128),
            place(10, 10, LOCAL, 384),
            place(8, 8, LOCAL, 1280),
            pltpu.VMEM((4, LOCAL, 384), F32),
            pltpu.VMEM((LOCAL, 2048), F32),
            pltpu.SemaphoreType.DMA((18,)),
        ],
        compiler_params=pltpu.CompilerParams(vmem_limit_bytes=67043328),
        cost_estimate=pl.CostEstimate(
            flops=19600000000, bytes_accessed=21000000, transcendentals=0
        ),
        name="network",
    )(*operands)


def cut(array, index, size, axis):
    return lax.dynamic_slice_in_dim(array, index * size, size, axis)


def statistics(message):
    highest = lax.Precision.HIGHEST
    x = lax.axis_index("xh") * 2 + lax.axis_index("xl")
    y = lax.axis_index("y")
    z = lax.axis_index("z")
    core = lax.axis_index("core")
    row_block = y * 4 + x
    col_block = z * 2 + core
    got = lax.all_to_all(message, ("xh", "xl", "z"), 0, 0, tiled=True)
    half_sum = jnp.sum(got[:, :, 896:], axis=0)
    shared = lax.dynamic_slice_in_dim(got, 128 * x, 128, 2)
    others = [got[:, :, 512 + 128 * n : 640 + 128 * n] for n in range(3)]
    rows = jnp.concatenate(
        [
            jnp.where(
                z == n, shared, jnp.where(n < z, others[min(n, 2)], others[max(n - 1, 0)])
            )
            for n in range(4)
        ],
        axis=-1,
    )
    other_columns = lax.dynamic_slice_in_dim(got, 256 * (1 - core), 256, 2)
    pass_on = jnp.concatenate([rows, other_columns], -1).reshape(256, 768)
    pass_on = jnp.concatenate([pass_on, jnp.pad(half_sum, ((0, 0), (0, 640)))], 0)
    passed = lax.ppermute(pass_on, "core", [(0, 1), (1, 0)])
    group_mean = (half_sum + passed[256:, :128]).reshape(FEAT) / GROUP
    own_columns = lax.dynamic_slice_in_dim(got, 256 * core, 256, 2).reshape(256, 256)
    rows_mean = lax.dynamic_index_in_dim(group_mean.reshape(4, 4, 128), x, 1, False).reshape(512)
    centered_rows = jnp.concatenate([rows.reshape(256, 512), passed[:256, :512]], 0) - rows_mean
    centered_columns = jnp.concatenate([own_columns, passed[:256, 512:]], 0) - cut(
        group_mean, col_block, 256, 0
    )
    moments = jnp.einsum(
        "nf,nc->fc",
        centered_rows,
        centered_columns,
        precision=highest,
        preferred_element_type=jnp.float32,
    )
    parts = jnp.concatenate(
        [
            moments.reshape(4, 128, 256),
            jnp.broadcast_to(group_mean.reshape(1, 8, 256), (4, 8, 256)),
        ],
        axis=1,
    )
    exchanged = [lax.dynamic_index_in_dim(parts, y, 0, False)]
    for n in (1, 3, 2):
        part = lax.dynamic_index_in_dim(parts, y ^ n, 0, False)
        exchanged.append(lax.ppermute(part, "y", [(k, k ^ n) for k in range(4)]))
    own, near, wrap, far = exchanged
    total = (own + near) + (far + wrap)
    feature_mean = total[128:].reshape(FEAT) / 4
    gap = jnp.stack([part[128:].reshape(FEAT) for part in exchanged]) - feature_mean
    between = jnp.einsum(
        "gf,gc->fc",
        cut(gap, row_block, 128, 1),
        cut(gap, col_block, 256, 1),
        precision=highest,
        preferred_element_type=jnp.float32,
    )
    covariance = (total[:128] + between * GROUP) / (IMAGES - 1)
    return feature_mean, covariance


def local(*arguments):
    return statistics(network(*arguments))


def solution(mesh):
    fine = Mesh(mesh.devices.reshape(4, 2, 2, 4, 2), AXES)
    placed = (P(AXES, None, None, None),) + (P(),) * 12
    return jax.shard_map(
        local,
        mesh=fine,
        in_specs=placed,
        out_specs=(P(), P(("y", "xh", "xl"), ("z", "core"))),
        check_vma=False,
    )
```

```python
import functools

import jax
import jax.numpy as jnp
from jax import lax
from jax.experimental import pallas as pl
from jax.experimental.pallas import tpu as pltpu
from jax.sharding import Mesh, PartitionSpec as P

AXES = ("y", "xh", "xl", "z", "core")
IMAGES = 2048
FEAT = 2048
LOCAL = 16
GROUP = 512


BF = jnp.bfloat16
F32 = jnp.float32


def relu(values):
    return jnp.maximum(values, 0.0).astype(BF)


def dot(a, b):
    return jnp.dot(a, b, preferred_element_type=F32)


def pack(taps, head, joint, tail):
    tiles = []

    def split(values):
        tiles.extend(values[:, c : c + 128] for c in range(0, values.shape[1], 128))

    for t in range(0, taps - 1, 2):
        split(head(t))
        tiles.append(joint(t, t + 1))
        split(tail(t + 1))
    split(head(taps - 1))
    tiles.append(joint(taps - 1, taps - 1)[:, :64])
    return tiles


def contract(tiles, weights, fillers=(), step=4):
    values, row = None, 0
    groups = range(0, len(tiles), step)
    for n, first in enumerate(groups):
        part = jnp.concatenate(tiles[first : first + step], axis=1)
        product = dot(part, weights[row : row + part.shape[1]])
        row += part.shape[1]
        values = product if values is None else values + product
        for filler in fillers[len(fillers) * n // len(groups) : len(fillers) * (n + 1) // len(groups)]:
            filler()
    return values


def network_kernel(
    x_hbm,
    entry_hbm,
    wide_hbm,
    row_hbm,
    column_hbm,
    reduce_hbm,
    second_hbm,
    second_row_hbm,
    second_column_hbm,
    second_deep_hbm,
    deep_row_hbm,
    deep_column_hbm,
    pool_hbm,
    out,
    x,
    entry_w,
    wide_w,
    row_w,
    column_w,
    reduce_w,
    second_w,
    second_deep_w,
    branch_w,
    pool_w,
    long_head,
    long_joint,
    long_tail,
    row_head,
    row_joint,
    row_tail,
    short_head,
    short_ends,
    short_tail,
    tower_head,
    tower_ends,
    tower_tail,
    middle,
    branch,
    deep_head,
    deep_last,
    deep_first,
    deep_tail,
    averaged,
    branch_sums,
    features,
    sems,
):
    def copy(name):
        source, target, slot = moves[name]
        return pltpu.make_async_copy(source, target, sems.at[slot])

    moves = {"entry": (entry_hbm, entry_w, 0)}
    copy("entry").start()
    def x_third(i, first):
        source = x_hbm.at[pl.ds(8 * i + first, 3)]
        target = x.at[pl.ds(9 * i + first, 3)]
        return pltpu.make_async_copy(source, target, sems.at[1 + 3 * i + first // 3])

    for i in range(2):
        for first in (0, 3, 6):
            x_third(i, first).start()

    def start_later():
        for name, _, _ in later:
            copy(name).start()

    later = [
        ("row", row_hbm, row_w),
        ("column", column_hbm, column_w),
        ("wide", wide_hbm, wide_w),
        ("reduce", reduce_hbm, reduce_w),
        ("second", second_hbm, second_w),
        ("second_deep", second_deep_hbm, second_deep_w),
        ("second_row", second_row_hbm, branch_w.at[0]),
        ("second_column", second_column_hbm, branch_w.at[1]),
        ("deep_row", deep_row_hbm, branch_w.at[2]),
        ("deep_column", deep_column_hbm, branch_w.at[3]),
        ("pool", pool_hbm, pool_w),
    ]
    for i, (name, source, target) in enumerate(later):
        moves[name] = (source, target, 7 + i)

    deep_last[...] = jnp.zeros((10, 10, LOCAL, 128), BF)
    deep_first[...] = jnp.zeros((10, 10, LOCAL, 128), BF)
    for array in (long_head, long_joint, long_tail):
        array[:, 0:3] = jnp.zeros((17, 3, LOCAL, 128), BF)
        array[:, 19:23] = jnp.zeros((17, 4, LOCAL, 128), BF)
    for array in (row_head, row_joint, row_tail):
        array[0:3] = jnp.zeros((3, 17, LOCAL, 128), BF)
        array[19:23] = jnp.zeros((4, 17, LOCAL, 128), BF)
    margins = [(middle, 1280), (deep_head, 384), (deep_tail, 384)]
    for array, channels in margins + [(branch.at[0], 384), (branch.at[1], 384)]:
        array[0] = jnp.zeros((10, LOCAL, channels), BF)
        array[9] = jnp.zeros((10, LOCAL, channels), BF)
        array[1:9, 0] = jnp.zeros((8, LOCAL, channels), BF)
        array[1:9, 9] = jnp.zeros((8, LOCAL, channels), BF)

    def split_by_parity(i, first, values, head, ends, tail):
        for r in range(first, first + 3):
            for c in range(17):
                at = (r % 2, c % 2, 4 * i + r // 2, c // 2)
                place = values[r - first, c]
                head[at] = place[:, 0:128]
                ends[(*at, slice(None), slice(0, 64))] = place[:, 128:192]
                ends[(*at, slice(None), slice(64, 128))] = place[:, 0:64]
                tail[at] = place[:, 64:192]

    def in_thirds(product, keep):
        earlier = product(0)
        for first in (3, 6):
            latter = product(first)
            keep(first - 3, earlier)
            earlier = latter
        keep(6, earlier)

    copy("entry").wait()

    def entry_block(i, carry):
        @pl.when(i == 1)
        def _():
            start_later()

        def product(first):
            x_third(i, first).wait()
            return dot(x[pl.ds(9 * i + first, 3)].reshape(816, 768), entry_w[...])

        def keep(first, values):
            values = relu(values).reshape(3, 17, LOCAL, 384)
            rows = pl.ds(8 * i + first, 3)
            long_head[rows, 3:20] = values[..., 192:320]
            long_joint[rows, 3:20, :, 0:64] = values[..., 320:384]
            long_joint[rows, 2:19, :, 64:128] = values[..., 192:256]
            long_tail[rows, 3:20] = values[..., 256:384]
            split_by_parity(i, first, values, short_head, short_ends, short_tail)

        in_thirds(product, keep)
        return carry

    lax.fori_loop(0, 2, entry_block, 0)

    copy("row").wait()

    def maximum(i, r):
        tall = [
            jnp.maximum(
                jnp.maximum(x[9 * i + 2 * r, c], x[9 * i + 2 * r + 1, c]), x[9 * i + 2 * r + 2, c]
            )
            for c in range(17)
        ]
        for c in range(8):
            middle[4 * i + r + 1, c + 1, :, 512:] = jnp.maximum(
                jnp.maximum(tall[2 * c], tall[2 * c + 1]), tall[2 * c + 2]
            )

    def row_block(i, carry):
        def at(array, t):
            return array[pl.ds(8 * i, 9), t : t + 17].reshape(2448, 128)

        tiles = pack(
            7,
            lambda t: at(long_head, t),
            lambda t, u: at(long_joint, t),
            lambda t: at(long_tail, t),
        )
        fillers = [functools.partial(maximum, i, r) for r in range(4)]
        values = relu(contract(tiles, row_w, fillers)).reshape(9, 17, LOCAL, 192)
        row_head[pl.ds(8 * i + 3, 9)] = values[..., 0:128]
        row_joint[pl.ds(8 * i + 3, 9), :, :, 0:64] = values[..., 128:192]
        row_joint[pl.ds(8 * i + 2, 9), :, :, 64:128] = values[..., 0:64]
        row_tail[pl.ds(8 * i + 3, 9)] = values[..., 64:192]
        return carry

    lax.fori_loop(0, 2, row_block, 0)
    copy("column").wait()

    def column_block(i, carry):
        def at(array, t):
            return array[pl.ds(8 * i + t, 9)].reshape(2448, 128)

        tiles = pack(
            7,
            lambda t: at(row_head, t),
            lambda t, u: at(row_joint, t),
            lambda t: at(row_tail, t),
        )
        values = relu(contract(tiles, column_w)).reshape(9, 17, LOCAL, 192)
        for first in (0, 3, 6):
            split_by_parity(
                i, first, values[first : first + 3], tower_head, tower_ends, tower_tail
            )
        return carry

    lax.fori_loop(0, 2, column_block, 0)
    copy("wide").wait()
    copy("reduce").wait()

    def half_map(step):
        lax.fori_loop(0, 2, lambda i, carry: step(4 * i), None)

    lower = lax.broadcasted_iota(jnp.int32, (512, 128), 1) < 64

    def joined(ends, t, u):
        return jnp.where(lower, ends(t), ends(u))

    def strided(arrays, weights, i):
        def at(array, t):
            a, b = t // 3, t % 3
            window = array[a % 2, b % 2, pl.ds(i + a // 2, 4), b // 2 : b // 2 + 8]
            return window.reshape(512, 128)

        head, ends, tail = (functools.partial(at, array) for array in arrays)
        return relu(contract(pack(9, head, functools.partial(joined, ends), tail), weights))

    def reduce_block(i):
        wide_out = strided((short_head, short_ends, short_tail), wide_w, i)
        middle[pl.ds(i + 1, 4), 1:9, :, 0:320] = wide_out.reshape(4, 8, LOCAL, 320)
        tower_out = strided((tower_head, tower_ends, tower_tail), reduce_w, i)
        middle[pl.ds(i + 1, 4), 1:9, :, 320:512] = tower_out.reshape(4, 8, LOCAL, 192)

    half_map(reduce_block)

    def add_sums(i, first, values):
        part = jnp.sum(values.astype(F32).reshape(32, LOCAL, -1), axis=0)
        at = slice(first, first + part.shape[1])
        features[:, at] = jnp.where(i == 0, 0.0, features[:, at]) + part

    copy("second").wait()

    def second_block(i):
        flat = middle[pl.ds(i + 1, 4), 1:9].reshape(512, 1280)
        second = relu(dot(flat, second_w[...]))
        add_sums(i, 0, second[:, 0:320])
        rows = pl.ds(i + 1, 4)
        branch[0, rows, 1:9] = second[:, 320:704].reshape(4, 8, LOCAL, 384)
        deep_head[rows, 1:9] = second[:, 704:1088].reshape(4, 8, LOCAL, 384)
        deep_last[rows, 1:9, :, 0:64] = second[:, 1088:1152].reshape(4, 8, LOCAL, 64)
        deep_first[rows, 1:9, :, 64:128] = second[:, 704:768].reshape(4, 8, LOCAL, 64)
        deep_tail[rows, 1:9] = second[:, 768:1152].reshape(4, 8, LOCAL, 384)

    half_map(second_block)

    copy("second_deep").wait()
    copy("pool").wait()

    def average(i, r, first):
        at = slice(first, first + 256)
        edge = i + r == (0 if r < 2 else 7)
        columns = [
            middle[i + r, j, :, at].astype(F32)
            + middle[i + r + 1, j, :, at].astype(F32)
            + middle[i + r + 2, j, :, at].astype(F32)
            for j in range(10)
        ]
        for j in range(8):
            width = 3 - (j == 0) - (j == 7)
            scale = jnp.where(edge, 1.0 / (2 * width), 1.0 / (3 * width))
            box = (columns[j] + columns[j + 1] + columns[j + 2]) * scale
            averaged[i + r, j, :, at] = box.astype(BF)

    def deep_block(i):
        def at(array, t):
            window = array[pl.ds(i + t // 3, 4), t % 3 : t % 3 + 8]
            return window.reshape(512, array.shape[3])

        tiles = pack(
            9,
            lambda t: at(deep_head, t),
            lambda t, u: at(deep_last, t) + at(deep_first, u),
            lambda t: at(deep_tail, t),
        )
        fillers = [functools.partial(average, i, r, 256 * n) for n in range(5) for r in range(4)]
        values = relu(contract(tiles, second_deep_w, fillers, 8))
        branch[1, pl.ds(i + 1, 4), 1:9] = values.reshape(4, 8, LOCAL, 384)
        pooled = lax.dot_general(
            averaged[pl.ds(i, 4)].reshape(512, 1280),
            pool_w[...],
            (((1,), (1,)), ((), ())),
            preferred_element_type=F32,
        )
        add_sums(i, 1856, relu(pooled))

    half_map(deep_block)
    for name in ("second_row", "second_column", "deep_row", "deep_column"):
        copy(name).wait()

    def branch_map(n, carry):
        def tap(t):
            down, right = jnp.where(n % 2 == 0, 1, t), jnp.where(n % 2 == 0, t, 1)
            return branch[n // 2, pl.ds(down, 8), pl.ds(right, 8)].reshape(1024, 384)

        values = relu(dot(jnp.concatenate([tap(t) for t in range(3)], axis=1), branch_w[n]))
        branch_sums[n] = jnp.sum(values.astype(F32).reshape(64, LOCAL, 384), axis=0)
        return carry

    lax.fori_loop(0, 4, branch_map, 0)
    for n in range(4):
        features[:, 320 + 384 * n : 704 + 384 * n] = branch_sums[n]
    for block in range(16):
        part = features[:, 128 * block : 128 * block + 128] * (1.0 / 64.0)
        total = jnp.sum(part, axis=0, keepdims=True)
        own_y, own_x = block // 4, block % 4
        for target in range(16):
            target_x, target_z = target // 4, target % 4
            slot = None
            if own_y == target_z:
                slot = own_x
            elif own_x == target_x:
                slot = 4 + own_y - (own_y > target_z)
            if slot is not None:
                out[target, :, 128 * slot : 128 * slot + 128] = part
            out[target, block : block + 1, 896:1024] = total


def network(
    block_inputs,
    first_entry,
    first_wide,
    first_row,
    first_column,
    first_reduce,
    second_entry,
    second_row,
    second_column,
    second_deep,
    deep_row,
    deep_column,
    pool_project,
):
    operands = (
        block_inputs.transpose(1, 2, 0, 3),
        first_entry[0, 0],
        first_wide.reshape(1728, 320),
        first_row.reshape(1344, 192),
        first_column.reshape(1344, 192),
        first_reduce.reshape(1728, 192),
        second_entry[0, 0],
        second_row.reshape(1152, 384),
        second_column.reshape(1152, 384),
        second_deep.reshape(4032, 384),
        deep_row.reshape(1152, 384),
        deep_column.reshape(1152, 384),
        pool_project[0, 0].T,
    )
    place = lambda *shape: pltpu.VMEM(shape, BF)
    return pl.pallas_call(
        network_kernel,
        out_shape=jax.ShapeDtypeStruct((16, LOCAL, 1024), F32),
        in_specs=[pl.BlockSpec(memory_space=pl.ANY)] * 13,
        out_specs=pl.BlockSpec(memory_space=pltpu.VMEM),
        scratch_shapes=[place(18, 17, LOCAL, 768)]
        + [place(*a.shape) for a in operands[1:7]]
        + [place(4032, 384), place(4, 1152, 384), place(192, 1280)]
        + [place(17, 23, LOCAL, 128)] * 3
        + [place(23, 17, LOCAL, 128)] * 3
        + [place(2, 2, 9, 9, LOCAL, 128)] * 6
        + [
            place(10, 10, LOCAL, 1280),
            place(2, 10, 10, LOCAL, 384),
            place(10, 10, LOCAL, 384),
            place(10, 10, LOCAL, 128),
            place(10, 10, LOCAL, 128),
            place(10, 10, LOCAL, 384),
            place(8, 8, LOCAL, 1280),
            pltpu.VMEM((4, LOCAL, 384), F32),
            pltpu.VMEM((LOCAL, 2048), F32),
            pltpu.SemaphoreType.DMA((18,)),
        ],
        compiler_params=pltpu.CompilerParams(vmem_limit_bytes=67043328),
        cost_estimate=pl.CostEstimate(
            flops=19600000000, bytes_accessed=21000000, transcendentals=0
        ),
        name="network",
    )(*operands)


def cut(array, index, size, axis):
    return lax.dynamic_slice_in_dim(array, index * size, size, axis)


def statistics(message):
    highest = lax.Precision.HIGHEST
    x = lax.axis_index("xh") * 2 + lax.axis_index("xl")
    y = lax.axis_index("y")
    z = lax.axis_index("z")
    core = lax.axis_index("core")
    row_block = y * 4 + x
    col_block = z * 2 + core
    got = lax.all_to_all(message, ("xh", "xl", "z"), 0, 0, tiled=True)
    half_sum = jnp.sum(got[:, :, 896:], axis=0)
    shared = lax.dynamic_slice_in_dim(got, 128 * x, 128, 2)
    others = [got[:, :, 512 + 128 * n : 640 + 128 * n] for n in range(3)]
    rows = jnp.concatenate(
        [
            jnp.where(
                z == n, shared, jnp.where(n < z, others[min(n, 2)], others[max(n - 1, 0)])
            )
            for n in range(4)
        ],
        axis=-1,
    )
    other_columns = lax.dynamic_slice_in_dim(got, 256 * (1 - core), 256, 2)
    pass_on = jnp.concatenate([rows, other_columns], -1).reshape(256, 768)
    pass_on = jnp.concatenate([pass_on, jnp.pad(half_sum, ((0, 0), (0, 640)))], 0)
    passed = lax.ppermute(pass_on, "core", [(0, 1), (1, 0)])
    group_mean = (half_sum + passed[256:, :128]).reshape(FEAT) / GROUP
    own_columns = lax.dynamic_slice_in_dim(got, 256 * core, 256, 2).reshape(256, 256)
    rows_mean = lax.dynamic_index_in_dim(group_mean.reshape(4, 4, 128), x, 1, False).reshape(512)
    centered_rows = jnp.concatenate([rows.reshape(256, 512), passed[:256, :512]], 0) - rows_mean
    centered_columns = jnp.concatenate([own_columns, passed[:256, 512:]], 0) - cut(
        group_mean, col_block, 256, 0
    )
    moments = jnp.einsum(
        "nf,nc->fc",
        centered_rows,
        centered_columns,
        precision=highest,
        preferred_element_type=jnp.float32,
    )
    parts = jnp.concatenate(
        [
            moments.reshape(4, 128, 256),
            jnp.broadcast_to(group_mean.reshape(1, 8, 256), (4, 8, 256)),
        ],
        axis=1,
    )
    exchanged = [lax.dynamic_index_in_dim(parts, y, 0, False)]
    for n in (1, 3, 2):
        part = lax.dynamic_index_in_dim(parts, (y + n) % 4, 0, False)
        exchanged.append(lax.ppermute(part, "y", [(k, (k + n) % 4) for k in range(4)]))
    own, before, after, across = exchanged
    total = (own + across) + (before + after)
    feature_mean = total[128:].reshape(FEAT) / 4
    gap = jnp.stack([part[128:].reshape(FEAT) for part in exchanged]) - feature_mean
    between = jnp.einsum(
        "gf,gc->fc",
        cut(gap, row_block, 128, 1),
        cut(gap, col_block, 256, 1),
        precision=highest,
        preferred_element_type=jnp.float32,
    )
    covariance = (total[:128] + between * GROUP) / (IMAGES - 1)
    return feature_mean, covariance


def local(*arguments):
    return statistics(network(*arguments))


def solution(mesh):
    fine = Mesh(mesh.devices.reshape(4, 2, 2, 4, 2), AXES)
    placed = (P(AXES, None, None, None),) + (P(),) * 12
    return jax.shard_map(
        local,
        mesh=fine,
        in_specs=placed,
        out_specs=(P(), P(("y", "xh", "xl"), ("z", "core"))),
        check_vma=False,
    )
```

```python
import functools

import jax
import jax.numpy as jnp
from jax import lax
from jax.experimental import pallas as pl
from jax.experimental.pallas import tpu as pltpu
from jax.sharding import Mesh, PartitionSpec as P

AXES = ("y", "xh", "xl", "z", "core")
IMAGES = 2048
FEAT = 2048
LOCAL = 16
GROUP = 512


BF = jnp.bfloat16
F32 = jnp.float32


def relu(values):
    return jnp.maximum(values, 0.0).astype(BF)


def dot(a, b):
    return jnp.dot(a, b, preferred_element_type=F32)


def pack(taps, head, joint, tail):
    tiles = []

    def split(values):
        tiles.extend(values[:, c : c + 128] for c in range(0, values.shape[1], 128))

    for t in range(0, taps - 1, 2):
        split(head(t))
        tiles.append(joint(t, t + 1))
        split(tail(t + 1))
    split(head(taps - 1))
    tiles.append(joint(taps - 1, taps - 1)[:, :64])
    return tiles


def contract(tiles, weights, fillers=(), step=4):
    values, row = None, 0
    groups = range(0, len(tiles), step)
    for n, first in enumerate(groups):
        part = jnp.concatenate(tiles[first : first + step], axis=1)
        product = dot(part, weights[row : row + part.shape[1]])
        row += part.shape[1]
        values = product if values is None else values + product
        for filler in fillers[len(fillers) * n // len(groups) : len(fillers) * (n + 1) // len(groups)]:
            filler()
    return values


def network_kernel(
    x_hbm,
    entry_hbm,
    wide_hbm,
    row_hbm,
    column_hbm,
    reduce_hbm,
    second_hbm,
    second_row_hbm,
    second_column_hbm,
    second_deep_hbm,
    deep_row_hbm,
    deep_column_hbm,
    pool_hbm,
    out,
    x,
    entry_w,
    wide_w,
    row_w,
    column_w,
    reduce_w,
    second_w,
    second_deep_w,
    branch_w,
    pool_w,
    long_head,
    long_joint,
    long_tail,
    row_head,
    row_joint,
    row_tail,
    short_head,
    short_ends,
    short_tail,
    tower_head,
    tower_ends,
    tower_tail,
    middle,
    branch,
    deep_head,
    deep_last,
    deep_first,
    deep_tail,
    averaged,
    branch_sums,
    features,
    sems,
):
    def copy(name):
        source, target, slot = moves[name]
        return pltpu.make_async_copy(source, target, sems.at[slot])

    moves = {"entry": (entry_hbm, entry_w, 0)}
    copy("entry").start()
    thirds = [(0, 3), (3, 3), (6, 3), (9, 3), (12, 3), (15, 2)]

    def x_rows(first, count):
        source, target = x_hbm.at[pl.ds(first, count)], x.at[pl.ds(first, count)]
        return pltpu.make_async_copy(source, target, sems.at[1 + first // 3])

    for first, count in thirds:
        x_rows(first, count).start()

    def start_later():
        for name, _, _ in later:
            copy(name).start()

    later = [
        ("row", row_hbm, row_w),
        ("column", column_hbm, column_w),
        ("wide", wide_hbm, wide_w),
        ("reduce", reduce_hbm, reduce_w),
        ("second", second_hbm, second_w),
        ("second_deep", second_deep_hbm, second_deep_w),
        ("second_row", second_row_hbm, branch_w.at[0]),
        ("second_column", second_column_hbm, branch_w.at[1]),
        ("deep_row", deep_row_hbm, branch_w.at[2]),
        ("deep_column", deep_column_hbm, branch_w.at[3]),
        ("pool", pool_hbm, pool_w),
    ]
    for i, (name, source, target) in enumerate(later):
        moves[name] = (source, target, 7 + i)
    start_later()

    deep_last[...] = jnp.zeros((10, 10, LOCAL, 128), BF)
    deep_first[...] = jnp.zeros((10, 10, LOCAL, 128), BF)
    for array in (long_head, long_joint, long_tail):
        array[:, 0:3] = jnp.zeros((17, 3, LOCAL, 128), BF)
        array[:, 19:23] = jnp.zeros((17, 4, LOCAL, 128), BF)
    for array in (row_head, row_joint, row_tail):
        array[0:3] = jnp.zeros((3, 17, LOCAL, 128), BF)
        array[19:23] = jnp.zeros((4, 17, LOCAL, 128), BF)
    margins = [(middle, 1280), (deep_head, 384), (deep_tail, 384)]
    for array, channels in margins + [(branch.at[0], 384), (branch.at[1], 384)]:
        array[0] = jnp.zeros((10, LOCAL, channels), BF)
        array[9] = jnp.zeros((10, LOCAL, channels), BF)
        array[1:9, 0] = jnp.zeros((8, LOCAL, channels), BF)
        array[1:9, 9] = jnp.zeros((8, LOCAL, channels), BF)

    def split_by_parity(i, first, values, head, ends, tail):
        for r in range(first, first + values.shape[0]):
            for c in range(17):
                at = (r % 2, c % 2, 4 * i + r // 2, c // 2)
                place = values[r - first, c]
                head[at] = place[:, 0:128]
                ends[(*at, slice(None), slice(0, 64))] = place[:, 128:192]
                ends[(*at, slice(None), slice(64, 128))] = place[:, 0:64]
                tail[at] = place[:, 64:192]

    copy("entry").wait()

    def entry_product(first, count):
        x_rows(first, count).wait()
        return dot(x[first : first + count].reshape(count * 272, 768), entry_w[...])

    def keep_entry(first, count, values):
        values = relu(values).reshape(count, 17, LOCAL, 384)
        rows = slice(first, first + count)
        long_head[rows, 3:20] = values[..., 192:320]
        long_joint[rows, 3:20, :, 0:64] = values[..., 320:384]
        long_joint[rows, 2:19, :, 64:128] = values[..., 192:256]
        long_tail[rows, 3:20] = values[..., 256:384]
        split_by_parity(0, first, values, short_head, short_ends, short_tail)

    earlier = None
    for first, count in thirds:
        latter = entry_product(first, count)
        if earlier is not None:
            keep_entry(*earlier)
        earlier = (first, count, latter)
    keep_entry(*earlier)

    copy("row").wait()

    def maximum(i, r):
        tall = [
            jnp.maximum(
                jnp.maximum(x[8 * i + 2 * r, c], x[8 * i + 2 * r + 1, c]), x[8 * i + 2 * r + 2, c]
            )
            for c in range(17)
        ]
        for c in range(8):
            middle[4 * i + r + 1, c + 1, :, 512:] = jnp.maximum(
                jnp.maximum(tall[2 * c], tall[2 * c + 1]), tall[2 * c + 2]
            )

    def row_product(first, count, fillers):
        def at(array, t):
            return array[first : first + count, t : t + 17].reshape(count * 272, 128)

        tiles = pack(
            7,
            lambda t: at(long_head, t),
            lambda t, u: at(long_joint, t),
            lambda t: at(long_tail, t),
        )
        return contract(tiles, row_w, fillers)

    def keep_row(first, count, values):
        values = relu(values).reshape(count, 17, LOCAL, 192)
        row_head[first + 3 : first + 3 + count] = values[..., 0:128]
        row_joint[first + 3 : first + 3 + count, :, :, 0:64] = values[..., 128:192]
        row_joint[first + 2 : first + 2 + count, :, :, 64:128] = values[..., 0:64]
        row_tail[first + 3 : first + 3 + count] = values[..., 64:192]

    fillers = [functools.partial(maximum, r // 4, r % 4) for r in range(8)]
    upper = row_product(0, 9, fillers[:4])
    lower_rows = row_product(9, 8, fillers[4:])
    keep_row(0, 9, upper)
    keep_row(9, 8, lower_rows)
    copy("column").wait()

    def column_product(first, count):
        def at(array, t):
            return array[first + t : first + t + count].reshape(count * 272, 128)

        tiles = pack(
            7,
            lambda t: at(row_head, t),
            lambda t, u: at(row_joint, t),
            lambda t: at(row_tail, t),
        )
        return contract(tiles, column_w)

    def keep_column(first, count, values):
        values = relu(values).reshape(count, 17, LOCAL, 192)
        split_by_parity(0, first, values, tower_head, tower_ends, tower_tail)

    upper = column_product(0, 9)
    lower_rows = column_product(9, 8)
    keep_column(0, 9, upper)
    keep_column(9, 8, lower_rows)
    copy("wide").wait()
    copy("reduce").wait()

    def half_map(step):
        lax.fori_loop(0, 2, lambda i, carry: step(4 * i), None)

    lower = lax.broadcasted_iota(jnp.int32, (512, 128), 1) < 64

    def joined(ends, t, u):
        return jnp.where(lower, ends(t), ends(u))

    def strided(arrays, weights, i):
        def at(array, t):
            a, b = t // 3, t % 3
            window = array[a % 2, b % 2, pl.ds(i + a // 2, 4), b // 2 : b // 2 + 8]
            return window.reshape(512, 128)

        head, ends, tail = (functools.partial(at, array) for array in arrays)
        return relu(contract(pack(9, head, functools.partial(joined, ends), tail), weights))

    def reduce_block(i):
        tower_out = strided((tower_head, tower_ends, tower_tail), reduce_w, i)
        wide_out = strided((short_head, short_ends, short_tail), wide_w, i)
        middle[pl.ds(i + 1, 4), 1:9, :, 0:320] = wide_out.reshape(4, 8, LOCAL, 320)
        middle[pl.ds(i + 1, 4), 1:9, :, 320:512] = tower_out.reshape(4, 8, LOCAL, 192)

    half_map(reduce_block)

    def add_sums(i, first, values):
        part = jnp.sum(values.astype(F32).reshape(32, LOCAL, -1), axis=0)
        at = slice(first, first + part.shape[1])
        features[:, at] = jnp.where(i == 0, 0.0, features[:, at]) + part

    copy("second").wait()

    def second_product(i):
        return dot(middle[i + 1 : i + 5, 1:9].reshape(512, 1280), second_w[...])

    def keep_second(i, values):
        second = relu(values)
        add_sums(i, 0, second[:, 0:320])
        rows = pl.ds(i + 1, 4)
        branch[0, rows, 1:9] = second[:, 320:704].reshape(4, 8, LOCAL, 384)
        deep_head[rows, 1:9] = second[:, 704:1088].reshape(4, 8, LOCAL, 384)
        deep_last[rows, 1:9, :, 0:64] = second[:, 1088:1152].reshape(4, 8, LOCAL, 64)
        deep_first[rows, 1:9, :, 64:128] = second[:, 704:768].reshape(4, 8, LOCAL, 64)
        deep_tail[rows, 1:9] = second[:, 768:1152].reshape(4, 8, LOCAL, 384)

    upper, lower_half = second_product(0), second_product(4)
    keep_second(0, upper)
    keep_second(4, lower_half)

    copy("second_deep").wait()
    copy("pool").wait()

    def average(i, r, first):
        at = slice(first, first + 256)
        edge = i + r == (0 if r < 2 else 7)
        columns = [
            middle[i + r, j, :, at].astype(F32)
            + middle[i + r + 1, j, :, at].astype(F32)
            + middle[i + r + 2, j, :, at].astype(F32)
            for j in range(10)
        ]
        for j in range(8):
            width = 3 - (j == 0) - (j == 7)
            scale = jnp.where(edge, 1.0 / (2 * width), 1.0 / (3 * width))
            box = (columns[j] + columns[j + 1] + columns[j + 2]) * scale
            averaged[i + r, j, :, at] = box.astype(BF)

    def deep_block(i):
        def at(array, t):
            window = array[pl.ds(i + t // 3, 4), t % 3 : t % 3 + 8]
            return window.reshape(512, array.shape[3])

        tiles = pack(
            9,
            lambda t: at(deep_head, t),
            lambda t, u: at(deep_last, t) + at(deep_first, u),
            lambda t: at(deep_tail, t),
        )
        fillers = [functools.partial(average, i, r, 256 * n) for n in range(5) for r in range(4)]
        values = relu(contract(tiles, second_deep_w, fillers, 8))
        branch[1, pl.ds(i + 1, 4), 1:9] = values.reshape(4, 8, LOCAL, 384)
        pooled = lax.dot_general(
            averaged[pl.ds(i, 4)].reshape(512, 1280),
            pool_w[...],
            (((1,), (1,)), ((), ())),
            preferred_element_type=F32,
        )
        add_sums(i, 1856, relu(pooled))

    half_map(deep_block)
    for name in ("second_row", "second_column", "deep_row", "deep_column"):
        copy(name).wait()

    def branch_pair(n, carry):
        def tap(down, right):
            return branch[n, pl.ds(down, 8), pl.ds(right, 8)].reshape(1024, 384)

        def product(taps, kind):
            return dot(jnp.concatenate(taps, axis=1), branch_w[2 * n + kind])

        def keep(values, kind):
            values = relu(values).astype(F32).reshape(64, LOCAL, 384)
            branch_sums[2 * n + kind] = jnp.sum(values, axis=0)

        across = product([tap(1, t) for t in range(3)], 0)
        down = product([tap(t, 1) for t in range(3)], 1)
        keep(across, 0)
        keep(down, 1)
        return carry

    lax.fori_loop(0, 2, branch_pair, 0)
    for n in range(4):
        features[:, 320 + 384 * n : 704 + 384 * n] = branch_sums[n]
    for block in range(16):
        part = features[:, 128 * block : 128 * block + 128] * (1.0 / 64.0)
        total = jnp.sum(part, axis=0, keepdims=True)
        own_y, own_x = block // 4, block % 4
        for target in range(16):
            target_x, target_z = target // 4, target % 4
            slot = None
            if own_y == target_z:
                slot = own_x
            elif own_x == target_x:
                slot = 4 + own_y - (own_y > target_z)
            if slot is not None:
                out[target, :, 128 * slot : 128 * slot + 128] = part
            out[target, block : block + 1, 896:1024] = total


def network(
    block_inputs,
    first_entry,
    first_wide,
    first_row,
    first_column,
    first_reduce,
    second_entry,
    second_row,
    second_column,
    second_deep,
    deep_row,
    deep_column,
    pool_project,
):
    operands = (
        block_inputs.transpose(1, 2, 0, 3),
        first_entry[0, 0],
        first_wide.reshape(1728, 320),
        first_row.reshape(1344, 192),
        first_column.reshape(1344, 192),
        first_reduce.reshape(1728, 192),
        second_entry[0, 0],
        second_row.reshape(1152, 384),
        second_column.reshape(1152, 384),
        second_deep.reshape(4032, 384),
        deep_row.reshape(1152, 384),
        deep_column.reshape(1152, 384),
        pool_project[0, 0].T,
    )
    place = lambda *shape: pltpu.VMEM(shape, BF)
    return pl.pallas_call(
        network_kernel,
        out_shape=jax.ShapeDtypeStruct((16, LOCAL, 1024), F32),
        in_specs=[pl.BlockSpec(memory_space=pl.ANY)] * 13,
        out_specs=pl.BlockSpec(memory_space=pltpu.VMEM),
        scratch_shapes=[place(17, 17, LOCAL, 768)]
        + [place(*a.shape) for a in operands[1:7]]
        + [place(4032, 384), place(4, 1152, 384), place(192, 1280)]
        + [place(17, 23, LOCAL, 128)] * 3
        + [place(23, 17, LOCAL, 128)] * 3
        + [place(2, 2, 9, 9, LOCAL, 128)] * 6
        + [
            place(10, 10, LOCAL, 1280),
            place(2, 10, 10, LOCAL, 384),
            place(10, 10, LOCAL, 384),
            place(10, 10, LOCAL, 128),
            place(10, 10, LOCAL, 128),
            place(10, 10, LOCAL, 384),
            place(8, 8, LOCAL, 1280),
            pltpu.VMEM((4, LOCAL, 384), F32),
            pltpu.VMEM((LOCAL, 2048), F32),
            pltpu.SemaphoreType.DMA((18,)),
        ],
        compiler_params=pltpu.CompilerParams(vmem_limit_bytes=67043328),
        cost_estimate=pl.CostEstimate(
            flops=19600000000, bytes_accessed=21000000, transcendentals=0
        ),
        name="network",
    )(*operands)


def cut(array, index, size, axis):
    return lax.dynamic_slice_in_dim(array, index * size, size, axis)


def statistics(message):
    highest = lax.Precision.HIGHEST
    x = lax.axis_index("xh") * 2 + lax.axis_index("xl")
    y = lax.axis_index("y")
    z = lax.axis_index("z")
    core = lax.axis_index("core")
    row_block = y * 4 + x
    col_block = z * 2 + core
    got = lax.all_to_all(message, ("xh", "xl", "z"), 0, 0, tiled=True)
    half_sum = jnp.sum(got[:, :, 896:], axis=0)
    shared = lax.dynamic_slice_in_dim(got, 128 * x, 128, 2)
    others = [got[:, :, 512 + 128 * n : 640 + 128 * n] for n in range(3)]
    rows = jnp.concatenate(
        [
            jnp.where(
                z == n, shared, jnp.where(n < z, others[min(n, 2)], others[max(n - 1, 0)])
            )
            for n in range(4)
        ],
        axis=-1,
    )
    other_columns = lax.dynamic_slice_in_dim(got, 256 * (1 - core), 256, 2)
    pass_on = jnp.concatenate([rows, other_columns], -1).reshape(256, 768)
    pass_on = jnp.concatenate([pass_on, jnp.pad(half_sum, ((0, 0), (0, 640)))], 0)
    passed = lax.ppermute(pass_on, "core", [(0, 1), (1, 0)])
    group_mean = (half_sum + passed[256:, :128]).reshape(FEAT) / GROUP
    own_columns = lax.dynamic_slice_in_dim(got, 256 * core, 256, 2).reshape(256, 256)
    rows_mean = lax.dynamic_index_in_dim(group_mean.reshape(4, 4, 128), x, 1, False).reshape(512)
    centered_rows = jnp.concatenate([rows.reshape(256, 512), passed[:256, :512]], 0) - rows_mean
    centered_columns = jnp.concatenate([own_columns, passed[:256, 512:]], 0) - cut(
        group_mean, col_block, 256, 0
    )
    moments = jnp.einsum(
        "nf,nc->fc",
        centered_rows,
        centered_columns,
        precision=highest,
        preferred_element_type=jnp.float32,
    )
    parts = jnp.concatenate(
        [
            moments.reshape(4, 128, 256),
            jnp.broadcast_to(group_mean.reshape(1, 8, 256), (4, 8, 256)),
        ],
        axis=1,
    )
    exchanged = [lax.dynamic_index_in_dim(parts, y, 0, False)]
    for n in (1, 3, 2):
        part = lax.dynamic_index_in_dim(parts, (y + n) % 4, 0, False)
        exchanged.append(lax.ppermute(part, "y", [(k, (k + n) % 4) for k in range(4)]))
    own, before, after, across = exchanged
    total = (own + across) + (before + after)
    feature_mean = total[128:].reshape(FEAT) / 4
    gap = jnp.stack([part[128:].reshape(FEAT) for part in exchanged]) - feature_mean
    between = jnp.einsum(
        "gf,gc->fc",
        cut(gap, row_block, 128, 1),
        cut(gap, col_block, 256, 1),
        precision=highest,
        preferred_element_type=jnp.float32,
    )
    covariance = (total[:128] + between * GROUP) / (IMAGES - 1)
    return feature_mean, covariance


def local(*arguments):
    return statistics(network(*arguments))


def solution(mesh):
    fine = Mesh(mesh.devices.reshape(4, 2, 2, 4, 2), AXES)
    placed = (P(AXES, None, None, None),) + (P(),) * 12
    return jax.shard_map(
        local,
        mesh=fine,
        in_specs=placed,
        out_specs=(P(), P(("y", "xh", "xl"), ("z", "core"))),
        check_vma=False,
    )
```

```python
import functools

import jax
import jax.numpy as jnp
from jax import lax
from jax.experimental import pallas as pl
from jax.experimental.pallas import tpu as pltpu
from jax.sharding import Mesh, PartitionSpec as P

AXES = ("y", "xh", "xl", "z", "core")
IMAGES = 2048
FEAT = 2048
LOCAL = 16
GROUP = 512


BF = jnp.bfloat16
F32 = jnp.float32


def relu(values):
    return jnp.maximum(values, 0.0).astype(BF)


def dot(a, b):
    return jnp.dot(a, b, preferred_element_type=F32)


def pack(taps, head, joint, tail):
    tiles = []

    def split(values):
        tiles.extend(values[:, c : c + 128] for c in range(0, values.shape[1], 128))

    for t in range(0, taps - 1, 2):
        split(head(t))
        tiles.append(joint(t, t + 1))
        split(tail(t + 1))
    split(head(taps - 1))
    tiles.append(joint(taps - 1, taps - 1)[:, :64])
    return tiles


def contract(tiles, weights, fillers=(), step=4):
    values, row = None, 0
    groups = range(0, len(tiles), step)
    for n, first in enumerate(groups):
        part = jnp.concatenate(tiles[first : first + step], axis=1)
        product = dot(part, weights[row : row + part.shape[1]])
        row += part.shape[1]
        values = product if values is None else values + product
        for filler in fillers[len(fillers) * n // len(groups) : len(fillers) * (n + 1) // len(groups)]:
            filler()
    return values


def network_kernel(
    x_hbm,
    entry_hbm,
    wide_hbm,
    row_hbm,
    column_hbm,
    reduce_hbm,
    second_hbm,
    second_row_hbm,
    second_column_hbm,
    second_deep_hbm,
    deep_row_hbm,
    deep_column_hbm,
    pool_hbm,
    out,
    x,
    entry_w,
    wide_w,
    row_w,
    column_w,
    reduce_w,
    second_w,
    second_deep_w,
    branch_w,
    pool_w,
    long_head,
    long_joint,
    long_tail,
    row_head,
    row_joint,
    row_tail,
    short_head,
    short_ends,
    short_tail,
    tower_head,
    tower_ends,
    tower_tail,
    middle,
    branch,
    deep_head,
    deep_last,
    deep_first,
    deep_tail,
    averaged,
    branch_sums,
    features,
    sems,
):
    def copy(name):
        source, target, slot = moves[name]
        return pltpu.make_async_copy(source, target, sems.at[slot])

    moves = {"entry": (entry_hbm, entry_w, 0)}
    copy("entry").start()
    thirds = [(0, 3), (3, 3), (6, 3), (9, 3), (12, 3), (15, 2)]

    def x_rows(first, count):
        source, target = x_hbm.at[pl.ds(first, count)], x.at[pl.ds(first, count)]
        return pltpu.make_async_copy(source, target, sems.at[1 + first // 3])

    for first, count in thirds:
        x_rows(first, count).start()

    def start_later():
        for name, _, _ in later:
            copy(name).start()

    later = [
        ("row", row_hbm, row_w),
        ("column", column_hbm, column_w),
        ("wide", wide_hbm, wide_w),
        ("reduce", reduce_hbm, reduce_w),
        ("second", second_hbm, second_w),
        ("second_deep", second_deep_hbm, second_deep_w),
        ("second_row", second_row_hbm, branch_w.at[0]),
        ("second_column", second_column_hbm, branch_w.at[1]),
        ("deep_row", deep_row_hbm, branch_w.at[2]),
        ("deep_column", deep_column_hbm, branch_w.at[3]),
        ("pool", pool_hbm, pool_w),
    ]
    for i, (name, source, target) in enumerate(later):
        moves[name] = (source, target, 7 + i)
    start_later()

    deep_last[...] = jnp.zeros((10, 10, LOCAL, 128), BF)
    deep_first[...] = jnp.zeros((10, 10, LOCAL, 128), BF)
    for array in (long_head, long_joint, long_tail):
        array[:, 0:3] = jnp.zeros((17, 3, LOCAL, 128), BF)
        array[:, 19:23] = jnp.zeros((17, 4, LOCAL, 128), BF)
    for array in (row_head, row_joint, row_tail):
        array[0:3] = jnp.zeros((3, 17, LOCAL, 128), BF)
        array[19:23] = jnp.zeros((4, 17, LOCAL, 128), BF)
    margins = [(middle, 1280), (deep_head, 384), (deep_tail, 384)]
    for array, channels in margins + [(branch.at[0], 384), (branch.at[1], 384)]:
        array[0] = jnp.zeros((10, LOCAL, channels), BF)
        array[9] = jnp.zeros((10, LOCAL, channels), BF)
        array[1:9, 0] = jnp.zeros((8, LOCAL, channels), BF)
        array[1:9, 9] = jnp.zeros((8, LOCAL, channels), BF)

    def split_by_parity(i, first, values, head, ends, tail):
        for r in range(first, first + values.shape[0]):
            for c in range(17):
                at = (r % 2, c % 2, 4 * i + r // 2, c // 2)
                place = values[r - first, c]
                head[at] = place[:, 0:128]
                ends[(*at, slice(None), slice(0, 64))] = place[:, 128:192]
                ends[(*at, slice(None), slice(64, 128))] = place[:, 0:64]
                tail[at] = place[:, 64:192]

    copy("entry").wait()

    def entry_product(first, count):
        x_rows(first, count).wait()
        return dot(x[first : first + count].reshape(count * 272, 768), entry_w[...])

    def keep_entry(first, count, values):
        values = relu(values).reshape(count, 17, LOCAL, 384)
        rows = slice(first, first + count)
        long_head[rows, 3:20] = values[..., 192:320]
        long_joint[rows, 3:20, :, 0:64] = values[..., 320:384]
        long_joint[rows, 2:19, :, 64:128] = values[..., 192:256]
        long_tail[rows, 3:20] = values[..., 256:384]
        split_by_parity(0, first, values, short_head, short_ends, short_tail)

    earlier = None
    for first, count in thirds:
        latter = entry_product(first, count)
        if earlier is not None:
            keep_entry(*earlier)
        earlier = (first, count, latter)
    keep_entry(*earlier)

    copy("row").wait()

    def maximum(i, r):
        tall = [
            jnp.maximum(
                jnp.maximum(x[8 * i + 2 * r, c], x[8 * i + 2 * r + 1, c]), x[8 * i + 2 * r + 2, c]
            )
            for c in range(17)
        ]
        for c in range(8):
            middle[4 * i + r + 1, c + 1, :, 512:] = jnp.maximum(
                jnp.maximum(tall[2 * c], tall[2 * c + 1]), tall[2 * c + 2]
            )

    def row_product(first, count, fillers):
        def at(array, t):
            return array[first : first + count, t : t + 17].reshape(count * 272, 128)

        tiles = pack(
            7,
            lambda t: at(long_head, t),
            lambda t, u: at(long_joint, t),
            lambda t: at(long_tail, t),
        )
        return contract(tiles, row_w, fillers)

    def keep_row(first, count, values):
        values = relu(values).reshape(count, 17, LOCAL, 192)
        row_head[first + 3 : first + 3 + count] = values[..., 0:128]
        row_joint[first + 3 : first + 3 + count, :, :, 0:64] = values[..., 128:192]
        row_joint[first + 2 : first + 2 + count, :, :, 64:128] = values[..., 0:64]
        row_tail[first + 3 : first + 3 + count] = values[..., 64:192]

    fillers = [functools.partial(maximum, r // 4, r % 4) for r in range(8)]
    upper = row_product(0, 9, fillers[:4])
    lower_rows = row_product(9, 8, fillers[4:])
    keep_row(0, 9, upper)
    keep_row(9, 8, lower_rows)
    copy("column").wait()

    def column_product(first, count):
        def at(array, t):
            return array[first + t : first + t + count].reshape(count * 272, 128)

        tiles = pack(
            7,
            lambda t: at(row_head, t),
            lambda t, u: at(row_joint, t),
            lambda t: at(row_tail, t),
        )
        return contract(tiles, column_w)

    def keep_column(first, count, values):
        values = relu(values).reshape(count, 17, LOCAL, 192)
        split_by_parity(0, first, values, tower_head, tower_ends, tower_tail)

    upper = column_product(0, 9)
    lower_rows = column_product(9, 8)
    keep_column(0, 9, upper)
    keep_column(9, 8, lower_rows)
    copy("wide").wait()
    copy("reduce").wait()

    def half_map(step):
        lax.fori_loop(0, 2, lambda i, carry: step(4 * i), None)

    lower = lax.broadcasted_iota(jnp.int32, (512, 128), 1) < 64

    def joined(ends, t, u):
        return jnp.where(lower, ends(t), ends(u))

    def strided(arrays, weights, i):
        def at(array, t):
            a, b = t // 3, t % 3
            window = array[a % 2, b % 2, pl.ds(i + a // 2, 4), b // 2 : b // 2 + 8]
            return window.reshape(512, 128)

        head, ends, tail = (functools.partial(at, array) for array in arrays)
        return relu(contract(pack(9, head, functools.partial(joined, ends), tail), weights))

    def reduce_block(i):
        tower_out = strided((tower_head, tower_ends, tower_tail), reduce_w, i)
        wide_out = strided((short_head, short_ends, short_tail), wide_w, i)
        middle[pl.ds(i + 1, 4), 1:9, :, 0:320] = wide_out.reshape(4, 8, LOCAL, 320)
        middle[pl.ds(i + 1, 4), 1:9, :, 320:512] = tower_out.reshape(4, 8, LOCAL, 192)

    half_map(reduce_block)

    def add_sums(i, first, values):
        part = jnp.sum(values.astype(F32).reshape(32, LOCAL, -1), axis=0)
        at = slice(first, first + part.shape[1])
        features[:, at] = jnp.where(i == 0, 0.0, features[:, at]) + part

    copy("second").wait()

    def second_product(i):
        return dot(middle[i + 1 : i + 5, 1:9].reshape(512, 1280), second_w[...])

    def keep_second(i, values):
        second = relu(values)
        add_sums(i, 0, second[:, 0:320])
        rows = pl.ds(i + 1, 4)
        branch[0, rows, 1:9] = second[:, 320:704].reshape(4, 8, LOCAL, 384)
        deep_head[rows, 1:9] = second[:, 704:1088].reshape(4, 8, LOCAL, 384)
        deep_last[rows, 1:9, :, 0:64] = second[:, 1088:1152].reshape(4, 8, LOCAL, 64)
        deep_first[rows, 1:9, :, 64:128] = second[:, 704:768].reshape(4, 8, LOCAL, 64)
        deep_tail[rows, 1:9] = second[:, 768:1152].reshape(4, 8, LOCAL, 384)

    upper, lower_half = second_product(0), second_product(4)
    keep_second(0, upper)
    keep_second(4, lower_half)

    copy("second_deep").wait()
    copy("pool").wait()

    def average(i, r, first):
        at = slice(first, first + 256)
        edge = i + r == (0 if r < 2 else 7)
        columns = [
            middle[i + r, j, :, at].astype(F32)
            + middle[i + r + 1, j, :, at].astype(F32)
            + middle[i + r + 2, j, :, at].astype(F32)
            for j in range(10)
        ]
        for j in range(8):
            width = 3 - (j == 0) - (j == 7)
            scale = jnp.where(edge, 1.0 / (2 * width), 1.0 / (3 * width))
            box = (columns[j] + columns[j + 1] + columns[j + 2]) * scale
            averaged[i + r, j, :, at] = box.astype(BF)

    def deep_block(i):
        def at(array, t):
            window = array[pl.ds(i + t // 3, 4), t % 3 : t % 3 + 8]
            return window.reshape(512, array.shape[3])

        tiles = pack(
            9,
            lambda t: at(deep_head, t),
            lambda t, u: at(deep_last, t) + at(deep_first, u),
            lambda t: at(deep_tail, t),
        )
        fillers = [functools.partial(average, i, r, 256 * n) for n in range(5) for r in range(4)]
        values = relu(contract(tiles, second_deep_w, fillers, 8))
        branch[1, pl.ds(i + 1, 4), 1:9] = values.reshape(4, 8, LOCAL, 384)
        pooled = lax.dot_general(
            averaged[pl.ds(i, 4)].reshape(512, 1280),
            pool_w[...],
            (((1,), (1,)), ((), ())),
            preferred_element_type=F32,
        )
        add_sums(i, 1856, relu(pooled))

    half_map(deep_block)
    for name in ("second_row", "second_column", "deep_row", "deep_column"):
        copy(name).wait()

    def branch_pair(n, carry):
        def tap(down, right):
            return branch[n, pl.ds(down, 8), pl.ds(right, 8)].reshape(1024, 384)

        def product(taps, kind):
            return dot(jnp.concatenate(taps, axis=1), branch_w[2 * n + kind])

        def keep(values, kind):
            values = relu(values).astype(F32).reshape(64, LOCAL, 384)
            branch_sums[2 * n + kind] = jnp.sum(values, axis=0)

        across = product([tap(1, t) for t in range(3)], 0)
        down = product([tap(t, 1) for t in range(3)], 1)
        keep(across, 0)
        keep(down, 1)
        return carry

    lax.fori_loop(0, 2, branch_pair, 0)
    for n in range(4):
        features[:, 320 + 384 * n : 704 + 384 * n] = branch_sums[n]
    for block in range(16):
        part = features[:, 128 * block : 128 * block + 128] * (1.0 / 64.0)
        total = jnp.sum(part, axis=0, keepdims=True)
        own_y, own_x = block // 4, block % 4
        for target in range(16):
            target_x, target_z = target // 4, target % 4
            slot = None
            if own_y == target_z:
                slot = own_x
            elif own_x == target_x:
                slot = 4 + own_y - (own_y > target_z)
            if slot is not None:
                out[target, :, 128 * slot : 128 * slot + 128] = part
            out[target, block : block + 1, 896:1024] = total


def network(
    block_inputs,
    first_entry,
    first_wide,
    first_row,
    first_column,
    first_reduce,
    second_entry,
    second_row,
    second_column,
    second_deep,
    deep_row,
    deep_column,
    pool_project,
):
    operands = (
        block_inputs.transpose(1, 2, 0, 3),
        first_entry[0, 0],
        first_wide.reshape(1728, 320),
        first_row.reshape(1344, 192),
        first_column.reshape(1344, 192),
        first_reduce.reshape(1728, 192),
        second_entry[0, 0],
        second_row.reshape(1152, 384),
        second_column.reshape(1152, 384),
        second_deep.reshape(4032, 384),
        deep_row.reshape(1152, 384),
        deep_column.reshape(1152, 384),
        pool_project[0, 0].T,
    )
    place = lambda *shape: pltpu.VMEM(shape, BF)
    return pl.pallas_call(
        network_kernel,
        out_shape=jax.ShapeDtypeStruct((16, LOCAL, 1024), F32),
        in_specs=[pl.BlockSpec(memory_space=pl.ANY)] * 13,
        out_specs=pl.BlockSpec(memory_space=pltpu.VMEM),
        scratch_shapes=[place(17, 17, LOCAL, 768)]
        + [place(*a.shape) for a in operands[1:7]]
        + [place(4032, 384), place(4, 1152, 384), place(192, 1280)]
        + [place(17, 23, LOCAL, 128)] * 3
        + [place(23, 17, LOCAL, 128)] * 3
        + [place(2, 2, 9, 9, LOCAL, 128)] * 6
        + [
            place(10, 10, LOCAL, 1280),
            place(2, 10, 10, LOCAL, 384),
            place(10, 10, LOCAL, 384),
            place(10, 10, LOCAL, 128),
            place(10, 10, LOCAL, 128),
            place(10, 10, LOCAL, 384),
            place(8, 8, LOCAL, 1280),
            pltpu.VMEM((4, LOCAL, 384), F32),
            pltpu.VMEM((LOCAL, 2048), F32),
            pltpu.SemaphoreType.DMA((18,)),
        ],
        compiler_params=pltpu.CompilerParams(vmem_limit_bytes=67043328),
        cost_estimate=pl.CostEstimate(
            flops=19600000000, bytes_accessed=21000000, transcendentals=0
        ),
        name="network",
    )(*operands)


def cut(array, index, size, axis):
    return lax.dynamic_slice_in_dim(array, index * size, size, axis)


def statistics(message):
    highest = lax.Precision.HIGHEST
    x = lax.axis_index("xh") * 2 + lax.axis_index("xl")
    y = lax.axis_index("y")
    z = lax.axis_index("z")
    core = lax.axis_index("core")
    row_block = y * 4 + x
    col_block = z * 2 + core
    got = lax.all_to_all(message, ("xh", "xl", "z"), 0, 0, tiled=True)
    half_sum = jnp.sum(got[:, :, 896:], axis=0)
    shared = lax.dynamic_slice_in_dim(got, 128 * x, 128, 2)
    others = [got[:, :, 512 + 128 * n : 640 + 128 * n] for n in range(3)]
    rows = jnp.concatenate(
        [
            jnp.where(
                z == n, shared, jnp.where(n < z, others[min(n, 2)], others[max(n - 1, 0)])
            )
            for n in range(4)
        ],
        axis=-1,
    )
    other_columns = lax.dynamic_slice_in_dim(got, 256 * (1 - core), 256, 2)
    pass_on = jnp.concatenate([rows, other_columns], -1).reshape(256, 768)
    pass_on = jnp.concatenate([pass_on, jnp.pad(half_sum, ((0, 0), (0, 640)))], 0)
    passed = lax.ppermute(pass_on, "core", [(0, 1), (1, 0)])
    group_mean = (half_sum + passed[256:, :128]).reshape(FEAT) / GROUP
    own_columns = lax.dynamic_slice_in_dim(got, 256 * core, 256, 2).reshape(256, 256)
    rows_mean = lax.dynamic_index_in_dim(group_mean.reshape(4, 4, 128), x, 1, False).reshape(512)
    centered_rows = jnp.concatenate([rows.reshape(256, 512), passed[:256, :512]], 0) - rows_mean
    centered_columns = jnp.concatenate([own_columns, passed[:256, 512:]], 0) - cut(
        group_mean, col_block, 256, 0
    )
    moments = jnp.einsum(
        "nf,nc->fc",
        centered_rows,
        centered_columns,
        precision=lax.Precision.HIGH,
        preferred_element_type=jnp.float32,
    )
    parts = jnp.concatenate(
        [
            moments.reshape(4, 128, 256),
            jnp.broadcast_to(group_mean.reshape(1, 8, 256), (4, 8, 256)),
        ],
        axis=1,
    )
    exchanged = [lax.dynamic_index_in_dim(parts, y, 0, False)]
    for n in (1, 3, 2):
        part = lax.dynamic_index_in_dim(parts, (y + n) % 4, 0, False)
        exchanged.append(lax.ppermute(part, "y", [(k, (k + n) % 4) for k in range(4)]))
    own, before, after, across = exchanged
    total = (own + across) + (before + after)
    feature_mean = total[128:].reshape(FEAT) / 4
    gap = jnp.stack([part[128:].reshape(FEAT) for part in exchanged]) - feature_mean
    between = jnp.einsum(
        "gf,gc->fc",
        cut(gap, row_block, 128, 1),
        cut(gap, col_block, 256, 1),
        precision=highest,
        preferred_element_type=jnp.float32,
    )
    covariance = (total[:128] + between * GROUP) / (IMAGES - 1)
    return feature_mean, covariance


def local(*arguments):
    return statistics(network(*arguments))


def solution(mesh):
    fine = Mesh(mesh.devices.reshape(4, 2, 2, 4, 2), AXES)
    placed = (P(AXES, None, None, None),) + (P(),) * 12
    return jax.shard_map(
        local,
        mesh=fine,
        in_specs=placed,
        out_specs=(P(), P(("y", "xh", "xl"), ("z", "core"))),
        check_vma=False,
    )
```
